32 devices in a mesh: dp: 4 (over y, x), seq: 4 (over z), fsdp: 2 (over core).
Axes of the slice: x: 2, y: 2, z: 4, core: 2. Of those that a mesh axis runs over, the one named last changes fastest.
Arguments:
- tokens: bfloat16 [4, 1024, 4096], P('dp', ('seq', 'fsdp')), may hold values from -6 to 6
- ffn_gain: float32 [4096], replicated, may hold values from 0.25 to 1.75
- in_proj: bfloat16 [4096, 16384], P(None, ('dp', 'seq', 'fsdp')), may hold values from -0.09375 to 0.09375
- out_proj: bfloat16 [16384, 4096], P(('dp', 'seq', 'fsdp')), may hold values from -0.046875 to 0.046875
- router_score: bfloat16 [4, 1024], P('dp', ('seq', 'fsdp')), may hold values from 0.25 to 2
- tile_counts: int32 [4, 8], P('dp', ('seq', 'fsdp')), may hold values from 1 to 12, 64 in all within a row
- tile_order: int32 [4, 8, 128], P('dp', ('seq', 'fsdp')), may hold values from 0 to 127, each once within a row
- light_qkv: bfloat16 [4, 1024, 3, 2048], P('dp', ('seq', 'fsdp')), may hold values from -16 to 16
- heavy_qkv: bfloat16 [4, 96, 3, 2048], P('dp', ('seq', 'fsdp')), may hold values from -16 to 16
Outputs:
- light_out: bfloat16 [4, 1024, 2048], P('dp', ('seq', 'fsdp'))
- heavy_attn: bfloat16 [4, 96, 2048], P('dp', ('seq', 'fsdp'))
- heavy_ffn: bfloat16 [4, 96, 4096], P('dp', ('seq', 'fsdp'))
The draws below stay inside these ranges and needn't reach their ends.
Inputs may be any that keep to these rules, and one draw needn't show every extreme that they name: `tile_counts`: each document's counts sum to 64; some tile of each document holds 12.
All inputs are finite; a program needn't handle non-finite values. No bound on the sum of `tile_counts` on one device may be relied on, other than what follows from the above.
Results may differ from the reference program's by a relative error of at most 0.02.
Values may be sent and summed in bfloat16 or wider, within the bound.
No kernel may reach another device: no remote copies, remote signals or barrier semaphores. Data moves between devices by JAX's collectives and lax.ppermute only.
A program may use at most 128 MiB of HBM per device.

```python
import math
import jax
import jax.numpy as jnp
import numpy as np
from jax import lax

D = 4096
FF = 16384
HEAD_DIM = 128
LIGHT_HEADS = 16
HEAVY_HEADS = 16
TILE = 128
CAP = 12
HALF_WIN = 64
DOCS = 4
LEN = 1024
TILES = 8
SLOTS = 96
ROUTED = 64


def draw_light_qkv(key, part):
    base = jax.random.normal(key, (DOCS, LEN, 3, LIGHT_HEADS * HEAD_DIM), jnp.float32)
    return jnp.clip(base, -16.0, 16.0).astype(jnp.bfloat16)


def draw_heavy_qkv(key, part):
    base = jax.random.normal(key, (DOCS, SLOTS, 3, HEAVY_HEADS * HEAD_DIM), jnp.float32)
    return jnp.clip(base, -16.0, 16.0).astype(jnp.bfloat16)


def block_levels(rng, shape, cuts, least, largest):
    factor_of = 1.0
    for dim, blocks in cuts:
        draws = jax.random.uniform(jax.random.fold_in(jax.random.fold_in(rng, 6), dim), (blocks,), jnp.float32, least / len(cuts), largest / len(cuts))
        factor_of = factor_of * jnp.repeat(jnp.exp(draws), shape[dim] // blocks).reshape((-1,) + (1,) * (len(shape) - 1 - dim))
    return factor_of


def split_up(amount, total, most, slope):
    loads = [(1 << 20) // math.isqrt(grade ** slope) + 1 for grade in range(2, amount + 1)]
    surplus, holding = total - most - (amount - 1), [1] * (amount - 1)
    while surplus > 0:
        movable = [i for i in range(amount - 1) if holding[i] < most]
        whole, left = sum([loads[i] for i in movable]), surplus
        for i in movable:
            more = min(most - holding[i], max(1, left * loads[i] // whole), surplus)
            holding[i] = holding[i] + more
            surplus = surplus - more
    return np.array([most] + holding)


def ragged(rng, count, total, limit, slope):
    if count == 2:
        one = jax.random.randint(rng, (), max(1, total - limit), min(limit, total - 1) + 1)
        return jnp.stack([one, total - one])
    lengths = jnp.asarray(split_up(count, total, limit, slope), jnp.int32)
    pairs = (count - 1) // 2
    giver, receiver = lengths[1:1 + 2 * pairs:2], lengths[2:2 + 2 * pairs:2]
    slack = jnp.minimum(giver - 1, limit - receiver)
    passed = jax.random.randint(jax.random.fold_in(rng, 1), (pairs,), 0, 1 << 20) % (slack + 1)
    lengths = lengths.at[1:1 + 2 * pairs:2].set(giver - passed).at[2:2 + 2 * pairs:2].set(receiver + passed)
    return lengths[jax.random.permutation(jax.random.fold_in(rng, 2), count)]


def bell_draw(key, dims, deviation, bound, shards=(), held_as=jnp.bfloat16):
    gain = block_levels(key, dims, shards, -0.22, 0.18) if shards else 1.0
    entries = jax.random.normal(key, dims, jnp.float32) * deviation * gain
    return jnp.minimum(jnp.maximum(entries, -bound), bound).astype(held_as)


def setup_inputs(seed: int = 0) -> dict:
    keys = jax.random.split(jax.random.key(seed), 10)
    return {
        "tokens": bell_draw(keys[0], (DOCS, LEN, D), 1.0, 6.0, ((0, 4), (1, 8))),
        "ffn_gain": jnp.clip(1.0 + 0.15 * jax.random.normal(keys[1], (D,), jnp.float32), 0.25, 1.75),
        "in_proj": bell_draw(keys[2], (D, FF), D ** -0.5, 0.09375, ((1, 32),)),
        "out_proj": bell_draw(keys[3], (FF, D), FF ** -0.5, 0.046875, ((0, 32),)),
        "router_score": jnp.clip(jnp.exp(math.log(2.0) - 2.0794415 * jax.random.uniform(keys[4], (DOCS, LEN), jnp.float32) ** block_levels(keys[4], (DOCS, LEN), ((0, 4), (1, 8)), -0.2, 0.2)), 0.25, 2.0).astype(jnp.bfloat16),
        "tile_counts": jax.vmap(lambda own: ragged(own, TILES, ROUTED, CAP, 2))(jax.random.split(keys[5], DOCS)).reshape((DOCS, TILES)).astype(jnp.int32),
        "tile_order": jax.vmap(lambda own: jax.random.permutation(own, TILE))(jax.random.split(keys[6], DOCS * TILES)).reshape((DOCS, TILES, TILE)).astype(jnp.int32),
        "light_qkv": draw_light_qkv(jax.random.fold_in(keys[9], 71), 0),
        "heavy_qkv": draw_heavy_qkv(jax.random.fold_in(keys[9], 71), 0),
    }


def masked_softmax_out(scores, usable, values):
    row_max = lax.optimization_barrier(jnp.max(jnp.where(usable, scores, -jnp.inf), axis=2, keepdims=True))
    expons = jnp.where(usable, jnp.exp(scores - row_max), 0.0)
    totals = lax.optimization_barrier(jnp.sum(expons, axis=2))
    rounded = lax.optimization_barrier(expons.astype(jnp.bfloat16)).astype(jnp.float32)
    return jnp.einsum('qhk,khd->qhd', rounded, values) / totals[:, :, None]

def light_document(qkv_doc):
    width = LIGHT_HEADS * HEAD_DIM
    queries = qkv_doc[:, 0].astype(jnp.float32).reshape(LEN, LIGHT_HEADS, HEAD_DIM)
    padded = jnp.pad(qkv_doc[:, 1:].astype(jnp.float32), ((HALF_WIN, HALF_WIN), (0, 0), (0, 0)))
    keys_all = padded[:, 0].reshape(LEN + 2 * HALF_WIN, LIGHT_HEADS, HEAD_DIM)
    values_all = padded[:, 1].reshape(LEN + 2 * HALF_WIN, LIGHT_HEADS, HEAD_DIM)
    span = TILE + 2 * HALF_WIN
    row_ids = jnp.arange(TILE).astype(jnp.int32)[:, None]
    col_ids = jnp.arange(span).astype(jnp.int32)[None, :]

    def block_out(block_index):
        begin = (block_index * TILE).astype(jnp.int32)
        query_rows = lax.dynamic_slice_in_dim(queries, begin, TILE, 0)
        key_rows = lax.dynamic_slice_in_dim(keys_all, begin, span, 0)
        value_rows = lax.dynamic_slice_in_dim(values_all, begin, span, 0)
        scores = jnp.einsum('qhd,khd->qhk', query_rows, key_rows) / math.sqrt(HEAD_DIM)
        positions = begin - HALF_WIN + col_ids
        inside = (col_ids >= row_ids) & (col_ids < row_ids + 2 * HALF_WIN) & (positions >= 0) & (positions < LEN)
        result = masked_softmax_out(scores, inside[:, None, :], value_rows)
        return result.reshape(TILE, width).astype(jnp.bfloat16)
    blocks = lax.map(block_out, jnp.arange(LEN // TILE).astype(jnp.int32))
    return blocks.reshape(LEN, width)

def heavy_document(qkv_doc, slot_live):
    width = HEAVY_HEADS * HEAD_DIM
    queries = qkv_doc[:, 0].astype(jnp.float32).reshape(SLOTS, HEAVY_HEADS, HEAD_DIM)
    keys_all = qkv_doc[:, 1].astype(jnp.float32).reshape(SLOTS, HEAVY_HEADS, HEAD_DIM)
    values_all = qkv_doc[:, 2].astype(jnp.float32).reshape(SLOTS, HEAVY_HEADS, HEAD_DIM)
    scores = jnp.einsum('qhd,khd->qhk', queries, keys_all) / math.sqrt(HEAD_DIM)
    result = masked_softmax_out(scores, slot_live[None, None, :], values_all)
    result = jnp.where(slot_live[:, None], result.reshape(SLOTS, width), 0.0)
    return result.astype(jnp.bfloat16)

def ffn_document(tokens_doc, ffn_gain, in_proj, out_proj, score_doc, counts_doc, order_doc):
    slot_row = (jnp.arange(TILES).astype(jnp.int32)[:, None] * TILE + order_doc[:, :CAP]).reshape(SLOTS).astype(jnp.int32)
    rows = jnp.take(tokens_doc, slot_row, axis=0).astype(jnp.float32)
    normed = (rows * lax.rsqrt(lax.optimization_barrier(jnp.mean(rows * rows, axis=1, keepdims=True)) + 1e-06) * ffn_gain).astype(jnp.bfloat16)
    slot_score = jnp.take(score_doc, slot_row).astype(jnp.float32)
    inclusive = jnp.cumsum(counts_doc).astype(jnp.int32)
    exclusive = (inclusive - counts_doc).astype(jnp.int32)
    positions = jnp.arange(ROUTED).astype(jnp.int32)
    tile_of = lax.optimization_barrier(jnp.sum((inclusive[None, :] <= positions[:, None]).astype(jnp.int32), axis=1)).astype(jnp.int32)
    source = (tile_of * CAP + positions - jnp.take(exclusive, tile_of)).astype(jnp.int32)
    compact = jnp.take(normed, source, axis=0)
    hidden = jnp.maximum(jnp.dot(compact, in_proj, preferred_element_type=jnp.float32), 0.0).astype(jnp.bfloat16)
    summed = jnp.dot(hidden, out_proj, preferred_element_type=jnp.float32)
    finished = (jnp.take(slot_score, source)[:, None] * summed).astype(jnp.bfloat16)
    ranks = jnp.arange(CAP).astype(jnp.int32)
    slot_live = (ranks[None, :] < counts_doc[:, None]).reshape(SLOTS)
    target = jnp.clip(exclusive[:, None] + ranks[None, :], 0, ROUTED - 1).reshape(SLOTS).astype(jnp.int32)
    picked = jnp.take(finished, target, axis=0)
    return jnp.where(slot_live[:, None], picked, jnp.zeros_like(picked))

def reference(tokens, ffn_gain, in_proj, out_proj, router_score, tile_counts, tile_order, light_qkv, heavy_qkv):
    light_list = []
    attn_list = []
    ffn_list = []
    ranks = jnp.arange(CAP).astype(jnp.int32)
    for doc_index in range(DOCS):
        slot_live = (ranks[None, :] < tile_counts[doc_index][:, None]).reshape(SLOTS)
        light_list.append(light_document(light_qkv[doc_index]))
        attn_list.append(heavy_document(heavy_qkv[doc_index], slot_live))
        ffn_list.append(ffn_document(tokens[doc_index], ffn_gain, in_proj, out_proj, router_score[doc_index], tile_counts[doc_index], tile_order[doc_index]))
    return (jnp.stack(light_list), jnp.stack(attn_list), jnp.stack(ffn_list))
```

```python
import functools
import math

import jax
import jax.numpy as jnp
from jax import lax
from jax.experimental import pallas as pl
from jax.experimental.pallas import tpu as pltpu
from jax.sharding import PartitionSpec as P

HEAD_DIM = 128
LIGHT_HEADS = 16
HEAVY_HEADS = 16
TILE = 128
CAP = 12
MEAN_LIVE = 8
HALF_WIN = 64
MARK = 1048576.0
F32, BF16 = jnp.float32, jnp.bfloat16
VMEM = pl.BlockSpec(memory_space=pltpu.VMEM)
SMEM = pl.BlockSpec(memory_space=pltpu.SMEM)


def iota(shape, dim):
    return lax.broadcasted_iota(jnp.int32, shape, dim)


def call(body, outs, args, scalars, flops, **kw):
    size = sum(math.prod(a.shape) * a.dtype.itemsize for a in (*args, *outs))
    return pl.pallas_call(
        body,
        out_shape=outs,
        in_specs=[SMEM] * scalars + [VMEM] * (len(args) - scalars),
        out_specs=[VMEM] * len(outs),
        cost_estimate=pl.CostEstimate(flops=flops, bytes_accessed=size, transcendentals=0),
        **kw,
    )(*args)


def struct(shape, dtype=BF16):
    return jax.ShapeDtypeStruct(shape, dtype)


def swap_core(x):
    return lax.ppermute(x, "fsdp", [(0, 1), (1, 0)])


def swap_seq(x, mask):
    n = lax.axis_size("seq")
    return lax.ppermute(x, "seq", [(i, i ^ mask) for i in range(n)])


def swap_doc(x, first):
    masks = (2, 1) if first else (1, 2)
    pairs = [(2 * d + c, 2 * (d ^ masks[c]) + c) for d in range(lax.axis_size("dp")) for c in range(2)]
    return lax.ppermute(x, ("dp", "fsdp"), pairs)


def seq_stages():
    n, stride, out = lax.axis_size("seq"), 1, []
    while stride < n:
        radix = min(4, n // stride)
        out.append((stride, radix))
        stride *= radix
    return out


def gather_seq(x):
    parts = [x]
    for stride, radix in seq_stages():
        x = jnp.concatenate(parts, axis=0) if len(parts) > 1 else parts[0]
        parts = [x] + [swap_seq(x, k * stride) for k in range(1, radix)]
    return parts


def scatter_seq(parts):
    stages = seq_stages()
    for at in range(len(stages) - 1, -1, -1):
        stride, radix = stages[at]
        total = parts[0].astype(F32)
        for k in range(1, radix):
            total = total + swap_seq(parts[k], k * stride).astype(F32)
        total = total.astype(BF16)
        if at:
            parts = jnp.split(total, stages[at - 1][1], axis=0)
    return total


def slot_rows_of(order_ref, rows, shift):
    lanes = iota((rows, TILE), 1)
    wanted = iota((rows, TILE), 0) - shift
    order = jnp.broadcast_to(order_ref[...], (rows, TILE))
    return jnp.sum(jnp.where(lanes == wanted, order, 0), axis=1, keepdims=True)


def pick_kernel(core_ref, count_ref, tokens_ref, order_ref, gain_ref, mine_ref, send_ref, all_ref):
    rows, half = mine_ref.shape
    core = core_ref[0]
    shift = core * CAP
    slot = iota((rows, 1), 0) - shift
    own = (slot >= 0) & (slot < CAP)
    picker = (slot_rows_of(order_ref, rows, shift) == iota((rows, TILE), 1)) & own
    x = jnp.dot(picker.astype(BF16), tokens_ref[...], preferred_element_type=F32)
    scale = lax.rsqrt(jnp.mean(x * x, axis=1, keepdims=True) + 1e-06)
    dead = own & (slot >= count_ref[0, 0])
    all_ref[...] = jnp.where(dead, MARK, x * scale * gain_ref[...]).astype(BF16)
    mine_ref[...] = all_ref[:, pl.ds(pl.multiple_of(core * half, 128), half)]
    send_ref[...] = all_ref[:, pl.ds(pl.multiple_of((1 - core) * half, 128), half)]


def pick_rows(core, counts, tokens, order, gain):
    rows, width = 2 * CAP, tokens.shape[1]
    return call(
        pick_kernel,
        [struct((rows, width // 2))] * 2,
        [core, counts, tokens, order, gain],
        2,
        2 * rows * TILE * width,
        scratch_shapes=[pltpu.VMEM((rows, width), BF16)],
    )


def compact_kernel(parts, *refs):
    ins, (out_ref, place_ref) = refs[:parts], refs[parts:]
    live_rows, width = out_ref.shape
    n = ins[0].shape[0]
    up, side = iota((n, n), 0), iota((n, n), 1)
    base = jnp.zeros((1, 1), F32)
    total = jnp.zeros((live_rows, width), F32)
    for k, ref in enumerate(ins):
        live = jnp.where(ref[:, 0:128].astype(F32)[:, 0:1] < MARK / 2, 1.0, 0.0)
        live_row = jnp.sum(jnp.where(up == side, live, 0.0), axis=0, keepdims=True)
        ahead_row = jnp.sum(jnp.where(up < side, live, 0.0), axis=0, keepdims=True) + base
        ahead = jnp.sum(jnp.where(side < up, live_row, 0.0), axis=1, keepdims=True) + base
        to_row = iota((live_rows, n), 0).astype(F32) == ahead_row
        pick = jnp.where(to_row & (live_row > 0.5), 1.0, 0.0).astype(BF16)
        total = total + jnp.dot(pick, ref[...], preferred_element_type=F32)
        at = iota((n, live_rows), 1).astype(F32) == ahead
        place_ref[k, :, :] = jnp.where(at & (live > 0.5), 1.0, 0.0).astype(BF16)
        base = base + jnp.sum(live, axis=0, keepdims=True)
    out_ref[...] = total.astype(BF16)


def compact(parts, live_rows):
    n, width = parts[0].shape
    return call(
        functools.partial(compact_kernel, len(parts)),
        [struct((live_rows, width)), struct((len(parts), n, live_rows))],
        parts,
        0,
        2 * len(parts) * n * live_rows * width,
    )


def spread_kernel(parts, place_ref, rows_ref, *outs):
    for k in range(parts):
        outs[k][...] = jnp.dot(
            place_ref[k, :, :], rows_ref[...], preferred_element_type=F32
        ).astype(BF16)


def spread(place, rows):
    parts, n, live_rows = place.shape
    width = rows.shape[1]
    return call(
        functools.partial(spread_kernel, parts),
        [struct((n, width))] * parts,
        [place, rows],
        0,
        2 * parts * n * live_rows * width,
    )


def ffn_kernel(core_ref, *refs):
    mine, peer, (win_ref, wout_ref), send, keep = (
        refs[0:4],
        refs[4:8],
        refs[8:10],
        refs[10:14],
        refs[14:18],
    )
    core = core_ref[0]
    rows, half = mine[0].shape
    units = win_ref.shape[1]
    at_mine = pl.multiple_of(core * half, 128)
    at_peer = pl.multiple_of((1 - core) * half, 128)
    group = max(1, min(4, 256 // rows))
    step = 256
    for first in range(0, 4, group):
        roles = range(first, first + group)
        x_mine = jnp.concatenate([mine[r][...] for r in roles], axis=0)
        x_peer = jnp.concatenate([peer[r][...] for r in roles], axis=0)
        total = jnp.dot(x_mine, win_ref[pl.ds(at_mine, half), :], preferred_element_type=F32)
        total = total + jnp.dot(x_peer, win_ref[pl.ds(at_peer, half), :], preferred_element_type=F32)
        hidden = jnp.maximum(total, 0.0).astype(BF16)

        def columns(i, carry, hidden=hidden, roles=roles):
            off = pl.multiple_of(i * step, step)
            for start, targets in ((at_peer, send), (at_mine, keep)):
                y = jnp.dot(
                    hidden, wout_ref[:, pl.ds(start + off, step)], preferred_element_type=F32
                ).astype(BF16)
                for j, r in enumerate(roles):
                    targets[r][:, pl.ds(off, step)] = y[j * rows : (j + 1) * rows]
            return carry

        lax.fori_loop(0, half // step, columns, 0)


def ffn(core, mine, peer, win, wout):
    rows, half = mine[0].shape
    units = win.shape[1]
    outs = call(
        ffn_kernel,
        [struct((rows, half))] * 8,
        [core, *mine, *peer, win, wout],
        1,
        4 * 4 * rows * 2 * half * units,
    )
    return outs[:4], outs[4:]


def finish_kernel(core_ref, count_ref, mine_ref, peer_ref, order_ref, score_ref, out_ref):
    rows, half = mine_ref.shape
    core = core_ref[0]
    pick = (iota((CAP, rows), 1) == iota((CAP, rows), 0) + core * CAP).astype(BF16)
    at = slot_rows_of(order_ref, CAP, 0) == iota((CAP, TILE), 1)
    score = jnp.sum(jnp.where(at, score_ref[...].astype(F32), 0.0), axis=1, keepdims=True)
    score = jnp.where(iota((CAP, 1), 0) < count_ref[0, 0], score, 0.0)
    for ref, start in ((mine_ref, core * half), (peer_ref, (1 - core) * half)):
        y = jnp.dot(pick, ref[...], preferred_element_type=F32)
        out_ref[:, pl.ds(pl.multiple_of(start, 128), half)] = (score * y).astype(BF16)


def finish(core, counts, mine, peer, order, score):
    rows, half = mine.shape
    return call(
        finish_kernel,
        [struct((CAP, 2 * half))],
        [core, counts, mine, peer, order, score],
        2,
        4 * CAP * rows * half,
    )[0]


def routed_ffn(core, tokens, gain, win, wout, score, counts, order):
    devices = lax.axis_size("seq") * lax.axis_size("fsdp")
    mine, send = pick_rows(core, counts, tokens, order, gain)
    pair = mine + swap_core(send)
    x0, place = compact(gather_seq(pair), MEAN_LIVE * devices)
    x1 = swap_doc(x0, True)
    x2 = swap_doc(x0, False)
    x3 = swap_doc(x1, False)
    mine = (x0, x1, x2, x3)
    p0, p2, p1, p3 = [swap_core(x) for x in mine]
    send, keep = ffn(core, mine, (p0, p1, p2, p3), win, wout)
    back = [swap_core(s) for s in send]

    def total(*terms):
        return sum(t.astype(F32) for t in terms).astype(BF16)

    got1 = swap_doc(total(keep[3], back[3]), True)
    got2 = swap_doc(total(keep[1], back[2]), True)
    got3 = swap_doc(total(keep[2], back[1], got1), False)
    own = total(keep[0], back[0], got2, got3)
    summed = scatter_seq(spread(place, own))
    return finish(core, counts, summed, swap_core(summed), order, score)


def light_kernel(info_ref, qkv_ref, far_ref, near_ref, out_ref):
    rows = qkv_ref.shape[1]
    core, first_pos, length = info_ref[0], info_ref[1], info_ref[2]
    span = rows + 2 * HALF_WIN
    lane = iota((rows, span), 1)
    row = iota((rows, span), 0)
    turn = jnp.where(core == 0, 0, rows + HALF_WIN)
    col = jnp.where(
        lane < HALF_WIN,
        lane + turn,
        jnp.where(lane < HALF_WIN + rows, lane, lane - turn),
    )
    pos = first_pos - HALF_WIN + col
    inside = (col >= row) & (col < row + 2 * HALF_WIN) & (pos >= 0) & (pos < length)
    bias = jnp.where(inside, 0.0, -1e30)
    for h in range(out_ref.shape[1] // HEAD_DIM):
        at = slice(h * HEAD_DIM, (h + 1) * HEAD_DIM)
        keys = jnp.concatenate([far_ref[0, :, at], qkv_ref[1, :, at], near_ref[0, :, at]], axis=0)
        values = jnp.concatenate([far_ref[1, :, at], qkv_ref[2, :, at], near_ref[1, :, at]], axis=0)
        s = lax.dot_general(
            qkv_ref[0, :, at], keys, (((1,), (1,)), ((), ())), preferred_element_type=F32
        )
        s = s * (1.0 / math.sqrt(HEAD_DIM)) + bias
        e = jnp.exp(s - jnp.max(s, axis=1, keepdims=True))
        y = jnp.dot(e.astype(BF16), values, preferred_element_type=F32)
        out_ref[:, at] = (y / jnp.sum(e, axis=1, keepdims=True)).astype(BF16)


def light_branch(core, qkv):
    rows, _, width = qkv.shape
    planes = jnp.transpose(qkv, (1, 0, 2))
    last = rows - HALF_WIN
    edge = core[0] * last
    far = lax.dynamic_slice(planes, (1, edge, 0), (2, HALF_WIN, width))
    near = lax.dynamic_slice(planes, (1, last - edge, 0), (2, HALF_WIN, width))
    n = lax.axis_size("seq") * lax.axis_size("fsdp")
    pairs = [(i, i + 1) for i in range(1, n - 1, 2)]
    far = lax.ppermute(far, ("seq", "fsdp"), pairs + [(j, i) for i, j in pairs])
    near = swap_core(near)
    first_pos = lax.axis_index(("seq", "fsdp")) * rows
    info = jnp.stack([core[0], first_pos, jnp.int32(n * rows)])
    wide = 4 * HEAD_DIM
    return pl.pallas_call(
        light_kernel,
        out_shape=struct((rows, width)),
        grid=(width // wide,),
        in_specs=[
            SMEM,
            pl.BlockSpec((3, rows, wide), lambda i: (0, 0, i)),
            pl.BlockSpec((2, HALF_WIN, wide), lambda i: (0, 0, i)),
            pl.BlockSpec((2, HALF_WIN, wide), lambda i: (0, 0, i)),
        ],
        out_specs=pl.BlockSpec((rows, wide), lambda i: (0, i)),
        cost_estimate=pl.CostEstimate(
            flops=4 * rows * 2 * rows * width,
            bytes_accessed=12 * rows * width,
            transcendentals=2 * rows * rows * LIGHT_HEADS,
        ),
    )(info, planes, far, near)


def heavy_kernel(q_ref, near_ref, far_ref, out_ref):
    rows, width = q_ref.shape
    n = 2 * near_ref.shape[0]
    kv = jnp.concatenate([near_ref[...], far_ref[...]], axis=0)
    first = (iota((8, HEAD_DIM), 1) == 0).astype(BF16)
    marks = lax.dot_general(
        first, kv[:, :HEAD_DIM], (((1,), (1,)), ((), ())), preferred_element_type=F32
    )[0:1]
    lane, row = iota((rows, n), 1), iota((rows, n), 0)
    same = (lax.rem(lane, 2 * CAP) < CAP) == (row < CAP)
    usable = same & (marks < MARK / 2)
    for h in range(width // HEAD_DIM):
        at = slice(h * HEAD_DIM, (h + 1) * HEAD_DIM)
        s = lax.dot_general(
            q_ref[:, at], kv[:, at], (((1,), (1,)), ((), ())), preferred_element_type=F32
        )
        s = jnp.where(usable, s * (1.0 / math.sqrt(HEAD_DIM)), -1e30)
        e = jnp.exp(s - jnp.max(s, axis=1, keepdims=True))
        y = jnp.dot(
            e.astype(BF16),
            kv[:, width + h * HEAD_DIM : width + (h + 1) * HEAD_DIM],
            preferred_element_type=F32,
        )
        out_ref[:, at] = (y / jnp.sum(e, axis=1, keepdims=True)).astype(BF16)


def heavy_branch(qkv, slot_live):
    slots, _, width = qkv.shape
    half = width // 2

    def stacked(x):
        return jnp.concatenate([x[:, :half], x[:, half:]], axis=0)

    q = stacked(qkv[:, 0])
    keys = jnp.where(slot_live[:, None], qkv[:, 1], jnp.bfloat16(MARK))
    kv = jnp.concatenate([stacked(keys), stacked(qkv[:, 2])], axis=1)
    near = jnp.concatenate(gather_seq(kv), axis=0)
    far = swap_core(near)
    out = call(
        heavy_kernel,
        [struct((2 * slots, half))],
        [q, near, far],
        0,
        4 * 2 * slots * 2 * near.shape[0] * half,
    )[0]
    out = jnp.concatenate([out[:slots], out[slots:]], axis=1)
    return jnp.where(slot_live[:, None], out, jnp.bfloat16(0))


def shards(
    tokens, ffn_gain, in_proj, out_proj, router_score, tile_counts, tile_order, light_qkv, heavy_qkv
):
    assert tile_order.shape[1] == 1 and lax.axis_size("fsdp") == 2 and lax.axis_size("dp") == 4
    core = lax.axis_index("fsdp").astype(jnp.int32).reshape(1)
    slot_live = jnp.arange(CAP) < tile_counts[0, 0]
    heavy_ffn = routed_ffn(
        core,
        tokens[0],
        ffn_gain[None],
        in_proj,
        out_proj,
        router_score,
        tile_counts,
        tile_order[0],
    )
    light_out = light_branch(core, light_qkv[0])
    heavy_attn = heavy_branch(heavy_qkv[0], slot_live)
    return (light_out[None], heavy_attn[None], heavy_ffn[None])


def solution(mesh):
    placed = (
        P("dp", ("seq", "fsdp"), None),
        P(),
        P(None, ("dp", "seq", "fsdp")),
        P(("dp", "seq", "fsdp"), None),
        P("dp", ("seq", "fsdp")),
        P("dp", ("seq", "fsdp")),
        P("dp", ("seq", "fsdp"), None),
        P("dp", ("seq", "fsdp"), None, None),
        P("dp", ("seq", "fsdp"), None, None),
    )
    return jax.shard_map(
        shards,
        mesh=mesh,
        in_specs=placed,
        out_specs=(
            P("dp", ("seq", "fsdp"), None),
            P("dp", ("seq", "fsdp"), None),
            P("dp", ("seq", "fsdp"), None),
        ),
        check_vma=False,
    )
```

```python
import functools
import math

import jax
import jax.numpy as jnp
from jax import lax
from jax.experimental import pallas as pl
from jax.experimental.pallas import tpu as pltpu
from jax.sharding import PartitionSpec as P


HEAD_DIM = 128
LIGHT_HEADS = 16
TILE = 128
CAP = 12
MEAN_LIVE = 8
HALF_WIN = 64
MARK = 1048576.0
F32, BF16 = jnp.float32, jnp.bfloat16
VMEM = pl.BlockSpec(memory_space=pltpu.VMEM)
SMEM = pl.BlockSpec(memory_space=pltpu.SMEM)


def iota(shape, dim):
    return lax.broadcasted_iota(jnp.int32, shape, dim)


def call(body, outs, args, scalars, flops, room=4 << 20, **kw):
    size = sum(math.prod(a.shape) * a.dtype.itemsize for a in (*args, *outs))
    return pl.pallas_call(
        body,
        out_shape=outs,
        in_specs=[SMEM] * scalars + [VMEM] * (len(args) - scalars),
        out_specs=[VMEM] * len(outs),
        cost_estimate=pl.CostEstimate(flops=flops, bytes_accessed=size, transcendentals=0),
        compiler_params=pltpu.CompilerParams(vmem_limit_bytes=min(60 << 20, size + room)),
        **kw,
    )(*args)


def struct(shape, dtype=BF16):
    return jax.ShapeDtypeStruct(shape, dtype)


def swap_core(x):
    return lax.ppermute(x, "fsdp", [(0, 1), (1, 0)])


def swap_seq(x, mask):
    n = lax.axis_size("seq")
    return lax.ppermute(x, "seq", [(i, i ^ mask) for i in range(n)])


def swap_doc(x, first):
    masks = (2, 1) if first else (1, 2)
    pairs = [(2 * d + c, 2 * (d ^ masks[c]) + c) for d in range(lax.axis_size("dp")) for c in range(2)]
    return lax.ppermute(x, ("dp", "fsdp"), pairs)


def seq_stages():
    n, stride, out = lax.axis_size("seq"), 1, []
    while stride < n:
        radix = min(4, n // stride)
        out.append((stride, radix))
        stride *= radix
    return out


def gather_seq(x):
    parts = [x]
    for stride, radix in seq_stages():
        x = jnp.concatenate(parts, axis=0) if len(parts) > 1 else parts[0]
        far = {k: swap_seq(x, k * stride) for k in range(radix - 1, 0, -1)}
        parts = [x] + [far[k] for k in range(1, radix)]
    return parts


def scatter_seq(parts):
    stages = seq_stages()
    for at in range(len(stages) - 1, -1, -1):
        stride, radix = stages[at]
        far = {k: swap_seq(parts[k], k * stride) for k in range(radix - 1, 0, -1)}
        total = parts[0].astype(F32)
        for k in range(1, radix):
            total = total + far[k].astype(F32)
        total = total.astype(BF16)
        if at:
            parts = jnp.split(total, stages[at - 1][1], axis=0)
    return total


def slot_rows_of(order_ref, rows, shift):
    lanes = iota((rows, TILE), 1)
    wanted = iota((rows, TILE), 0) - shift
    order = jnp.broadcast_to(order_ref[...], (rows, TILE))
    return jnp.sum(jnp.where(lanes == wanted, order, 0), axis=1, keepdims=True)


def pick_kernel(core_ref, count_ref, tokens_ref, order_ref, gain_ref, mine_ref, send_ref, all_ref):
    rows, half = mine_ref.shape
    core = core_ref[0]
    shift = core * CAP
    slot = iota((rows, 1), 0) - shift
    own = (slot >= 0) & (slot < CAP)
    picker = (slot_rows_of(order_ref, rows, shift) == iota((rows, TILE), 1)) & own
    x = jnp.dot(picker.astype(BF16), tokens_ref[...], preferred_element_type=F32)
    scale = lax.rsqrt(jnp.mean(x * x, axis=1, keepdims=True) + 1e-06)
    dead = own & (slot >= count_ref[0, 0])
    all_ref[...] = jnp.where(dead, MARK, x * scale * gain_ref[...]).astype(BF16)
    mine_ref[...] = all_ref[:, pl.ds(pl.multiple_of(core * half, 128), half)]
    send_ref[...] = all_ref[:, pl.ds(pl.multiple_of((1 - core) * half, 128), half)]


def pick_rows(core, counts, tokens, order, gain):
    rows, width = 2 * CAP, tokens.shape[1]
    return call(
        pick_kernel,
        [struct((rows, width // 2))] * 2,
        [core, counts, tokens, order, gain],
        2,
        2 * rows * TILE * width,
        scratch_shapes=[pltpu.VMEM((rows, width), BF16)],
    )


def compact_kernel(parts, *refs):
    ins, (out_ref, place_ref) = refs[:parts], refs[parts:]
    live_rows, width = out_ref.shape
    n = ins[0].shape[0]
    up, side = iota((n, n), 0), iota((n, n), 1)
    base = jnp.zeros((1, 1), F32)
    total = jnp.zeros((live_rows, width), F32)
    for k, ref in enumerate(ins):
        live = jnp.where(ref[:, 0:128].astype(F32)[:, 0:1] < MARK / 2, 1.0, 0.0)
        live_row = jnp.sum(jnp.where(up == side, live, 0.0), axis=0, keepdims=True)
        ahead_row = jnp.sum(jnp.where(up < side, live, 0.0), axis=0, keepdims=True) + base
        ahead = jnp.sum(jnp.where(side < up, live_row, 0.0), axis=1, keepdims=True) + base
        to_row = iota((live_rows, n), 0).astype(F32) == ahead_row
        pick = jnp.where(to_row & (live_row > 0.5), 1.0, 0.0).astype(BF16)
        total = total + jnp.dot(pick, ref[...], preferred_element_type=F32)
        at = iota((n, live_rows), 1).astype(F32) == ahead
        place_ref[k, :, :] = jnp.where(at & (live > 0.5), 1.0, 0.0).astype(BF16)
        base = base + jnp.sum(live, axis=0, keepdims=True)
    out_ref[...] = total.astype(BF16)


def compact(parts, live_rows):
    n, width = parts[0].shape
    return call(
        functools.partial(compact_kernel, len(parts)),
        [struct((live_rows, width)), struct((len(parts), n, live_rows))],
        parts,
        0,
        2 * len(parts) * n * live_rows * width,
    )


def spread_kernel(parts, place_ref, rows_ref, *outs):
    for k in range(parts):
        outs[k][...] = jnp.dot(
            place_ref[k, :, :], rows_ref[...], preferred_element_type=F32
        ).astype(BF16)


def spread(place, rows):
    parts, n, live_rows = place.shape
    width = rows.shape[1]
    return call(
        functools.partial(spread_kernel, parts),
        [struct((n, width))] * parts,
        [place, rows],
        0,
        2 * parts * n * live_rows * width,
    )


def ffn_kernel(core_ref, *refs):
    mine, peer, (win_ref, wout_ref), send, keep = (
        refs[0:4],
        refs[4:8],
        refs[8:10],
        refs[10:14],
        refs[14:18],
    )
    core = core_ref[0]
    rows, half = mine[0].shape
    at_mine = pl.multiple_of(core * half, 128)
    at_peer = pl.multiple_of((1 - core) * half, 128)
    group = max(1, min(4, 256 // rows))
    step = 256
    for first in range(0, 4, group):
        roles = range(first, first + group)
        x_mine = jnp.concatenate([mine[r][...] for r in roles], axis=0)
        x_peer = jnp.concatenate([peer[r][...] for r in roles], axis=0)
        total = jnp.dot(x_mine, win_ref[pl.ds(at_mine, half), :], preferred_element_type=F32)
        total = total + jnp.dot(x_peer, win_ref[pl.ds(at_peer, half), :], preferred_element_type=F32)
        hidden = jnp.maximum(total, 0.0).astype(BF16)

        def columns(i, carry, hidden=hidden, roles=roles):
            off = pl.multiple_of(i * step, step)
            for start, targets in ((at_peer, send), (at_mine, keep)):
                y = jnp.dot(
                    hidden, wout_ref[:, pl.ds(start + off, step)], preferred_element_type=F32
                ).astype(BF16)
                for j, r in enumerate(roles):
                    targets[r][:, pl.ds(off, step)] = y[j * rows : (j + 1) * rows]
            return carry

        lax.fori_loop(0, half // step, columns, 0)


def ffn(core, mine, peer, win, wout):
    rows, half = mine[0].shape
    units = win.shape[1]
    outs = call(
        ffn_kernel,
        [struct((rows, half))] * 8,
        [core, *mine, *peer, win, wout],
        1,
        4 * 4 * rows * 2 * half * units,
    )
    return outs[:4], outs[4:]


def finish_kernel(core_ref, count_ref, mine_ref, peer_ref, order_ref, score_ref, out_ref):
    rows, half = mine_ref.shape
    core = core_ref[0]
    pick = (iota((CAP, rows), 1) == iota((CAP, rows), 0) + core * CAP).astype(BF16)
    at = slot_rows_of(order_ref, CAP, 0) == iota((CAP, TILE), 1)
    score = jnp.sum(jnp.where(at, score_ref[...].astype(F32), 0.0), axis=1, keepdims=True)
    score = jnp.where(iota((CAP, 1), 0) < count_ref[0, 0], score, 0.0)
    for ref, start in ((mine_ref, core * half), (peer_ref, (1 - core) * half)):
        y = jnp.dot(pick, ref[...], preferred_element_type=F32)
        out_ref[:, pl.ds(pl.multiple_of(start, 128), half)] = (score * y).astype(BF16)


def finish(core, counts, mine, peer, order, score):
    rows, half = mine.shape
    return call(
        finish_kernel,
        [struct((CAP, 2 * half))],
        [core, counts, mine, peer, order, score],
        2,
        4 * CAP * rows * half,
    )[0]


def load_kernel(*refs):
    n = len(refs) // 2
    copies = [pltpu.make_async_copy(refs[i], refs[n + i], refs[2 * n].at[i]) for i in range(n)]
    for c in copies:
        c.start()
    for c in copies:
        c.wait()


def load(*arrays):
    n = len(arrays)
    return pl.pallas_call(
        load_kernel,
        out_shape=[struct(a.shape, a.dtype) for a in arrays],
        in_specs=[pl.BlockSpec(memory_space=pltpu.HBM)] * n,
        out_specs=[VMEM] * n,
        scratch_shapes=[pltpu.SemaphoreType.DMA((n,))],
        cost_estimate=pl.CostEstimate(
            flops=0, bytes_accessed=sum(2 * a.size for a in arrays), transcendentals=0
        ),
        compiler_params=pltpu.CompilerParams(
            vmem_limit_bytes=46 << 20
        ),
    )(*arrays)


def routed_ffn(core, tokens, gain, win, wout, score, counts, order, heavy_qkv):
    devices = lax.axis_size("seq") * lax.axis_size("fsdp")
    mine, send = pick_rows(core, counts, tokens, order, gain)
    pair = mine + swap_core(send)
    heavy_qkv, _ = lax.optimization_barrier((heavy_qkv, pair))
    win, wout = load(win, wout)
    x0, place = compact(gather_seq(pair), MEAN_LIVE * devices)
    x1 = swap_doc(x0, True)
    x2 = swap_doc(x0, False)
    x3 = swap_doc(x1, False)
    mine = (x0, x1, x2, x3)
    p0, p2, p1, p3 = [swap_core(x) for x in mine]
    send, keep = ffn(core, mine, (p0, p1, p2, p3), win, wout)
    back = {i: swap_core(send[i]) for i in (3, 2, 1, 0)}

    def total(*terms):
        return sum(t.astype(F32) for t in terms).astype(BF16)

    got1 = swap_doc(total(keep[3], back[3]), True)
    got2 = swap_doc(total(keep[1], back[2]), True)
    got3 = swap_doc(total(keep[2], back[1], got1), False)
    own = total(keep[0], back[0], got2, got3)
    summed = scatter_seq(spread(place, own))
    return finish(core, counts, summed, swap_core(summed), order, score), heavy_qkv


def light_kernel(info_ref, qkv_ref, far_ref, near_ref, out_ref):
    rows = qkv_ref.shape[1]
    core, first_pos, length = info_ref[0], info_ref[1], info_ref[2]
    span = rows + 2 * HALF_WIN
    lane = iota((rows, span), 1)
    row = iota((rows, span), 0)
    turn = jnp.where(core == 0, 0, rows + HALF_WIN)
    col = jnp.where(
        lane < HALF_WIN,
        lane + turn,
        jnp.where(lane < HALF_WIN + rows, lane, lane - turn),
    )
    pos = first_pos - HALF_WIN + col
    inside = (col >= row) & (col < row + 2 * HALF_WIN) & (pos >= 0) & (pos < length)
    bias = jnp.where(inside, 0.0, -1e30)
    for h in range(out_ref.shape[1] // HEAD_DIM):
        at = slice(h * HEAD_DIM, (h + 1) * HEAD_DIM)
        keys = jnp.concatenate([far_ref[0, :, at], qkv_ref[1, :, at], near_ref[0, :, at]], axis=0)
        values = jnp.concatenate([far_ref[1, :, at], qkv_ref[2, :, at], near_ref[1, :, at]], axis=0)
        s = lax.dot_general(
            qkv_ref[0, :, at], keys, (((1,), (1,)), ((), ())), preferred_element_type=F32
        )
        s = s * (1.0 / math.sqrt(HEAD_DIM)) + bias
        e = jnp.exp(s - jnp.max(s, axis=1, keepdims=True))
        y = jnp.dot(e.astype(BF16), values, preferred_element_type=F32)
        out_ref[:, at] = (y / jnp.sum(e, axis=1, keepdims=True)).astype(BF16)


def light_branch(core, qkv):
    rows, _, width = qkv.shape
    planes = jnp.transpose(qkv, (1, 0, 2))
    last = rows - HALF_WIN
    edge = core[0] * last
    far = lax.dynamic_slice(planes, (1, edge, 0), (2, HALF_WIN, width))
    near = lax.dynamic_slice(planes, (1, last - edge, 0), (2, HALF_WIN, width))
    n = lax.axis_size("seq") * lax.axis_size("fsdp")
    pairs = [(i, i + 1) for i in range(1, n - 1, 2)]
    far = lax.ppermute(far, ("seq", "fsdp"), pairs + [(j, i) for i, j in pairs])
    near = swap_core(near)
    first_pos = lax.axis_index(("seq", "fsdp")) * rows
    info = jnp.stack([core[0], first_pos, jnp.int32(n * rows)])
    wide = 4 * HEAD_DIM
    return pl.pallas_call(
        light_kernel,
        out_shape=struct((rows, width)),
        grid=(width // wide,),
        in_specs=[
            SMEM,
            pl.BlockSpec((3, rows, wide), lambda i: (0, 0, i)),
            pl.BlockSpec((2, HALF_WIN, wide), lambda i: (0, 0, i)),
            pl.BlockSpec((2, HALF_WIN, wide), lambda i: (0, 0, i)),
        ],
        out_specs=pl.BlockSpec((rows, wide), lambda i: (0, i)),
        cost_estimate=pl.CostEstimate(
            flops=4 * rows * 2 * rows * width,
            bytes_accessed=12 * rows * width,
            transcendentals=2 * rows * rows * LIGHT_HEADS,
        ),
        compiler_params=pltpu.CompilerParams(vmem_limit_bytes=12 << 20),
    )(info, planes, far, near)


def heavy_kernel(q_ref, near_ref, far_ref, out_ref):
    rows, width = q_ref.shape
    n = 2 * near_ref.shape[0]
    kv = jnp.concatenate([near_ref[...], far_ref[...]], axis=0)
    first = (iota((8, HEAD_DIM), 1) == 0).astype(BF16)
    marks = lax.dot_general(
        first, kv[:, :HEAD_DIM], (((1,), (1,)), ((), ())), preferred_element_type=F32
    )[0:1]
    lane, row = iota((rows, n), 1), iota((rows, n), 0)
    same = (lax.rem(lane, 2 * CAP) < CAP) == (row < CAP)
    usable = same & (marks < MARK / 2)
    for h in range(width // HEAD_DIM):
        at = slice(h * HEAD_DIM, (h + 1) * HEAD_DIM)
        s = lax.dot_general(
            q_ref[:, at], kv[:, at], (((1,), (1,)), ((), ())), preferred_element_type=F32
        )
        s = jnp.where(usable, s * (1.0 / math.sqrt(HEAD_DIM)), -1e30)
        e = jnp.exp(s - jnp.max(s, axis=1, keepdims=True))
        y = jnp.dot(
            e.astype(BF16),
            kv[:, width + h * HEAD_DIM : width + (h + 1) * HEAD_DIM],
            preferred_element_type=F32,
        )
        out_ref[:, at] = (y / jnp.sum(e, axis=1, keepdims=True)).astype(BF16)


def heavy_branch(qkv, slot_live):
    slots, _, width = qkv.shape
    half = width // 2

    def stacked(x):
        return jnp.concatenate([x[:, :half], x[:, half:]], axis=0)

    q = stacked(qkv[:, 0])
    keys = jnp.where(slot_live[:, None], qkv[:, 1], jnp.bfloat16(MARK))
    kv = jnp.concatenate([stacked(keys), stacked(qkv[:, 2])], axis=1)
    near = jnp.concatenate(gather_seq(kv), axis=0)
    far = swap_core(near)
    out = call(
        heavy_kernel,
        [struct((2 * slots, half))],
        [q, near, far],
        0,
        4 * 2 * slots * 2 * near.shape[0] * half,
    )[0]
    out = jnp.concatenate([out[:slots], out[slots:]], axis=1)
    return jnp.where(slot_live[:, None], out, jnp.bfloat16(0))


def layer(
    tokens, ffn_gain, in_proj, out_proj, router_score, tile_counts, tile_order, light_qkv, heavy_qkv
):
    assert tile_order.shape[1] == 1 and lax.axis_size("fsdp") == 2 and lax.axis_size("dp") == 4
    core = lax.axis_index("fsdp").astype(jnp.int32).reshape(1)
    slot_live = jnp.arange(CAP) < tile_counts[0, 0]
    heavy_ffn, heavy_qkv = routed_ffn(
        core,
        tokens[0],
        ffn_gain[None],
        in_proj,
        out_proj,
        router_score,
        tile_counts,
        tile_order[0],
        heavy_qkv,
    )
    light_out = light_branch(core, light_qkv[0])
    heavy_attn = heavy_branch(heavy_qkv[0], slot_live)
    return (light_out[None], heavy_attn[None], heavy_ffn[None])


def solution(mesh):
    placed = (
        P("dp", ("seq", "fsdp"), None),
        P(),
        P(None, ("dp", "seq", "fsdp")),
        P(("dp", "seq", "fsdp"), None),
        P("dp", ("seq", "fsdp")),
        P("dp", ("seq", "fsdp")),
        P("dp", ("seq", "fsdp"), None),
        P("dp", ("seq", "fsdp"), None, None),
        P("dp", ("seq", "fsdp"), None, None),
    )
    return jax.shard_map(
        layer,
        mesh=mesh,
        in_specs=placed,
        out_specs=(
            P("dp", ("seq", "fsdp"), None),
            P("dp", ("seq", "fsdp"), None),
            P("dp", ("seq", "fsdp"), None),
        ),
        check_vma=False,
    )
```

```python
import functools
import math

import jax
import jax.numpy as jnp
from jax import lax
from jax.experimental import pallas as pl
from jax.experimental.pallas import tpu as pltpu
from jax.sharding import PartitionSpec as P


HEAD_DIM = 128
LIGHT_HEADS = 16
TILE = 128
CAP = 12
MEAN_LIVE = 8
HALF_WIN = 64
MARK = 1048576.0
F32, BF16 = jnp.float32, jnp.bfloat16
VMEM = pl.BlockSpec(memory_space=pltpu.VMEM)
SMEM = pl.BlockSpec(memory_space=pltpu.SMEM)


def iota(shape, dim):
    return lax.broadcasted_iota(jnp.int32, shape, dim)


def call(body, outs, args, scalars, flops, room=4 << 20, **kw):
    size = sum(math.prod(a.shape) * a.dtype.itemsize for a in (*args, *outs))
    return pl.pallas_call(
        body,
        out_shape=outs,
        in_specs=[SMEM] * scalars + [VMEM] * (len(args) - scalars),
        out_specs=[VMEM] * len(outs),
        cost_estimate=pl.CostEstimate(flops=flops, bytes_accessed=size, transcendentals=0),
        compiler_params=pltpu.CompilerParams(vmem_limit_bytes=min(60 << 20, size + room)),
        **kw,
    )(*args)


def struct(shape, dtype=BF16):
    return jax.ShapeDtypeStruct(shape, dtype)


def swap_core(x):
    return lax.ppermute(x, "fsdp", [(0, 1), (1, 0)])


def swap_seq(x, mask):
    n = lax.axis_size("seq")
    return lax.ppermute(x, "seq", [(i, i ^ mask) for i in range(n)])


def swap_doc(x, first):
    masks = (2, 1) if first else (1, 2)
    pairs = [(2 * d + c, 2 * (d ^ masks[c]) + c) for d in range(lax.axis_size("dp")) for c in range(2)]
    return lax.ppermute(x, ("dp", "fsdp"), pairs)


def seq_stages():
    n, stride, out = lax.axis_size("seq"), 1, []
    while stride < n:
        radix = min(4, n // stride)
        out.append((stride, radix))
        stride *= radix
    return out


def gather_seq(x):
    parts = [x]
    for stride, radix in seq_stages():
        x = jnp.concatenate(parts, axis=0) if len(parts) > 1 else parts[0]
        far = {k: swap_seq(x, k * stride) for k in range(radix - 1, 0, -1)}
        parts = [x] + [far[k] for k in range(1, radix)]
    return parts


def scatter_seq(parts):
    stages = seq_stages()
    for at in range(len(stages) - 1, -1, -1):
        stride, radix = stages[at]
        far = {k: swap_seq(parts[k], k * stride) for k in range(radix - 1, 0, -1)}
        total = parts[0].astype(F32)
        for k in range(1, radix):
            total = total + far[k].astype(F32)
        total = total.astype(BF16)
        if at:
            parts = jnp.split(total, stages[at - 1][1], axis=0)
    return total


def slot_rows_of(order_ref, rows, shift):
    lanes = iota((rows, TILE), 1)
    wanted = iota((rows, TILE), 0) - shift
    order = jnp.broadcast_to(order_ref[...], (rows, TILE))
    return jnp.sum(jnp.where(lanes == wanted, order, 0), axis=1, keepdims=True)


def pick_kernel(core_ref, count_ref, tokens_ref, order_ref, gain_ref, mine_ref, send_ref, all_ref):
    rows, half = mine_ref.shape
    core = core_ref[0]
    shift = core * CAP
    slot = iota((rows, 1), 0) - shift
    own = (slot >= 0) & (slot < CAP)
    picker = (slot_rows_of(order_ref, rows, shift) == iota((rows, TILE), 1)) & own
    x = jnp.dot(picker.astype(BF16), tokens_ref[...], preferred_element_type=F32)
    scale = lax.rsqrt(jnp.mean(x * x, axis=1, keepdims=True) + 1e-06)
    dead = own & (slot >= count_ref[0, 0])
    all_ref[...] = jnp.where(dead, MARK, x * scale * gain_ref[...]).astype(BF16)
    mine_ref[...] = all_ref[:, pl.ds(pl.multiple_of(core * half, 128), half)]
    send_ref[...] = all_ref[:, pl.ds(pl.multiple_of((1 - core) * half, 128), half)]


def pick_rows(core, counts, tokens, order, gain):
    rows, width = 2 * CAP, tokens.shape[1]
    return call(
        pick_kernel,
        [struct((rows, width // 2))] * 2,
        [core, counts, tokens, order, gain],
        2,
        2 * rows * TILE * width,
        room=54 << 20,
        scratch_shapes=[pltpu.VMEM((rows, width), BF16)],
    )


def compact_kernel(parts, *refs):
    ins, (out_ref, place_ref) = refs[:parts], refs[parts:]
    live_rows, width = out_ref.shape
    n = ins[0].shape[0]
    up, side = iota((n, n), 0), iota((n, n), 1)
    base = jnp.zeros((1, 1), F32)
    total = jnp.zeros((live_rows, width), F32)
    for k, ref in enumerate(ins):
        live = jnp.where(ref[:, 0:128].astype(F32)[:, 0:1] < MARK / 2, 1.0, 0.0)
        live_row = jnp.sum(jnp.where(up == side, live, 0.0), axis=0, keepdims=True)
        ahead_row = jnp.sum(jnp.where(up < side, live, 0.0), axis=0, keepdims=True) + base
        ahead = jnp.sum(jnp.where(side < up, live_row, 0.0), axis=1, keepdims=True) + base
        to_row = iota((live_rows, n), 0).astype(F32) == ahead_row
        pick = jnp.where(to_row & (live_row > 0.5), 1.0, 0.0).astype(BF16)
        total = total + jnp.dot(pick, ref[...], preferred_element_type=F32)
        at = iota((n, live_rows), 1).astype(F32) == ahead
        place_ref[k, :, :] = jnp.where(at & (live > 0.5), 1.0, 0.0).astype(BF16)
        base = base + jnp.sum(live, axis=0, keepdims=True)
    out_ref[...] = total.astype(BF16)


def compact(parts, live_rows):
    n, width = parts[0].shape
    return call(
        functools.partial(compact_kernel, len(parts)),
        [struct((live_rows, width)), struct((len(parts), n, live_rows))],
        parts,
        0,
        2 * len(parts) * n * live_rows * width,
    )


def spread_kernel(parts, place_ref, rows_ref, *outs):
    for k in range(parts):
        outs[k][...] = jnp.dot(
            place_ref[k, :, :], rows_ref[...], preferred_element_type=F32
        ).astype(BF16)


def spread(place, rows):
    parts, n, live_rows = place.shape
    width = rows.shape[1]
    return call(
        functools.partial(spread_kernel, parts),
        [struct((n, width))] * parts,
        [place, rows],
        0,
        2 * parts * n * live_rows * width,
    )


def ffn_kernel(core_ref, *refs):
    mine, peer, (win_ref, wout_ref), send, keep = (
        refs[0:4],
        refs[4:8],
        refs[8:10],
        refs[10:14],
        refs[14:18],
    )
    core = core_ref[0]
    rows, half = mine[0].shape
    at_mine = pl.multiple_of(core * half, 128)
    at_peer = pl.multiple_of((1 - core) * half, 128)
    group = max(1, min(4, 256 // rows))
    step = 256
    for first in range(0, 4, group):
        roles = range(first, first + group)
        x_mine = jnp.concatenate([mine[r][...] for r in roles], axis=0)
        x_peer = jnp.concatenate([peer[r][...] for r in roles], axis=0)
        total = jnp.dot(x_mine, win_ref[pl.ds(at_mine, half), :], preferred_element_type=F32)
        total = total + jnp.dot(x_peer, win_ref[pl.ds(at_peer, half), :], preferred_element_type=F32)
        hidden = jnp.maximum(total, 0.0).astype(BF16)

        def columns(i, carry, hidden=hidden, roles=roles):
            off = pl.multiple_of(i * step, step)
            for start, targets in ((at_peer, send), (at_mine, keep)):
                y = jnp.dot(
                    hidden, wout_ref[:, pl.ds(start + off, step)], preferred_element_type=F32
                ).astype(BF16)
                for j, r in enumerate(roles):
                    targets[r][:, pl.ds(off, step)] = y[j * rows : (j + 1) * rows]
            return carry

        lax.fori_loop(0, half // step, columns, 0)


def ffn(core, mine, peer, win, wout):
    rows, half = mine[0].shape
    units = win.shape[1]
    outs = call(
        ffn_kernel,
        [struct((rows, half))] * 8,
        [core, *mine, *peer, win, wout],
        1,
        4 * 4 * rows * 2 * half * units,
    )
    return outs[:4], outs[4:]


def finish_kernel(core_ref, count_ref, mine_ref, peer_ref, order_ref, score_ref, out_ref):
    rows, half = mine_ref.shape
    core = core_ref[0]
    pick = (iota((CAP, rows), 1) == iota((CAP, rows), 0) + core * CAP).astype(BF16)
    at = slot_rows_of(order_ref, CAP, 0) == iota((CAP, TILE), 1)
    score = jnp.sum(jnp.where(at, score_ref[...].astype(F32), 0.0), axis=1, keepdims=True)
    score = jnp.where(iota((CAP, 1), 0) < count_ref[0, 0], score, 0.0)
    for ref, start in ((mine_ref, core * half), (peer_ref, (1 - core) * half)):
        y = jnp.dot(pick, ref[...], preferred_element_type=F32)
        out_ref[:, pl.ds(pl.multiple_of(start, 128), half)] = (score * y).astype(BF16)


def finish(core, counts, mine, peer, order, score):
    rows, half = mine.shape
    return call(
        finish_kernel,
        [struct((CAP, 2 * half))],
        [core, counts, mine, peer, order, score],
        2,
        4 * CAP * rows * half,
    )[0]


def load_kernel(*refs):
    n = len(refs) // 2
    copies = [pltpu.make_async_copy(refs[i], refs[n + i], refs[2 * n].at[i]) for i in range(n)]
    for c in copies:
        c.start()
    for c in copies:
        c.wait()


def load(*arrays):
    n = len(arrays)
    return pl.pallas_call(
        load_kernel,
        out_shape=[struct(a.shape, a.dtype) for a in arrays],
        in_specs=[pl.BlockSpec(memory_space=pltpu.HBM)] * n,
        out_specs=[VMEM] * n,
        scratch_shapes=[pltpu.SemaphoreType.DMA((n,))],
        cost_estimate=pl.CostEstimate(
            flops=0, bytes_accessed=sum(2 * a.size for a in arrays), transcendentals=0
        ),
        compiler_params=pltpu.CompilerParams(
            vmem_limit_bytes=42 << 20
        ),
    )(*arrays)


def routed_ffn(core, tokens, gain, win, wout, score, counts, order, heavy_qkv):
    devices = lax.axis_size("seq") * lax.axis_size("fsdp")
    mine, send = pick_rows(core, counts, tokens, order, gain)
    pair = mine + swap_core(send)
    heavy_qkv, _ = lax.optimization_barrier((heavy_qkv, pair))
    win, wout = load(win, wout)
    x0, place = compact(gather_seq(pair), MEAN_LIVE * devices)
    x1 = swap_doc(x0, True)
    x2 = swap_doc(x0, False)
    x3 = swap_doc(x1, False)
    mine = (x0, x1, x2, x3)
    p0, p2, p1, p3 = [swap_core(x) for x in mine]
    send, keep = ffn(core, mine, (p0, p1, p2, p3), win, wout)
    back = {i: swap_core(send[i]) for i in (3, 2, 1, 0)}

    def total(*terms):
        return sum(t.astype(F32) for t in terms).astype(BF16)

    got1 = swap_doc(total(keep[3], back[3]), True)
    got2 = swap_doc(total(keep[1], back[2]), True)
    got3 = swap_doc(total(keep[2], back[1], got1), False)
    own = total(keep[0], back[0], got2, got3)
    summed = scatter_seq(spread(place, own))
    return finish(core, counts, summed, swap_core(summed), order, score), heavy_qkv


def light_kernel(info_ref, qkv_ref, far_ref, near_ref, out_ref):
    rows = qkv_ref.shape[1]
    core, first_pos, length = info_ref[0], info_ref[1], info_ref[2]
    span = rows + 2 * HALF_WIN
    lane = iota((rows, span), 1)
    row = iota((rows, span), 0)
    turn = jnp.where(core == 0, 0, rows + HALF_WIN)
    col = jnp.where(
        lane < HALF_WIN,
        lane + turn,
        jnp.where(lane < HALF_WIN + rows, lane, lane - turn),
    )
    pos = first_pos - HALF_WIN + col
    inside = (col >= row) & (col < row + 2 * HALF_WIN) & (pos >= 0) & (pos < length)
    bias = jnp.where(inside, 0.0, -1e30)
    for h in range(out_ref.shape[1] // HEAD_DIM):
        at = slice(h * HEAD_DIM, (h + 1) * HEAD_DIM)
        keys = jnp.concatenate([far_ref[0, :, at], qkv_ref[1, :, at], near_ref[0, :, at]], axis=0)
        values = jnp.concatenate([far_ref[1, :, at], qkv_ref[2, :, at], near_ref[1, :, at]], axis=0)
        s = lax.dot_general(
            qkv_ref[0, :, at], keys, (((1,), (1,)), ((), ())), preferred_element_type=F32
        )
        s = s * (1.0 / math.sqrt(HEAD_DIM)) + bias
        e = jnp.exp(s - jnp.max(s, axis=1, keepdims=True))
        y = jnp.dot(e.astype(BF16), values, preferred_element_type=F32)
        out_ref[:, at] = (y / jnp.sum(e, axis=1, keepdims=True)).astype(BF16)


def halo_kernel(info_ref, planes_ref, far_ref, near_ref, sems):
    last = planes_ref.shape[1] - HALF_WIN
    edge = pl.multiple_of(info_ref[0] * last, HALF_WIN)
    other = pl.multiple_of(last - edge, HALF_WIN)
    copies = [
        pltpu.make_async_copy(planes_ref.at[1:3, pl.ds(at, HALF_WIN)], ref, sems.at[i])
        for i, (at, ref) in enumerate(((edge, far_ref), (other, near_ref)))
    ]
    for c in copies:
        c.start()
    for c in copies:
        c.wait()


def light_branch(info, planes):
    _, rows, width = planes.shape
    run = pl.pallas_call(
        halo_kernel,
        out_shape=[struct((2, HALF_WIN, width))] * 2,
        in_specs=[SMEM, pl.BlockSpec(memory_space=pl.ANY)],
        out_specs=[VMEM] * 2,
        scratch_shapes=[pltpu.SemaphoreType.DMA((2,))],
        cost_estimate=pl.CostEstimate(
            flops=0, bytes_accessed=8 * HALF_WIN * width, transcendentals=0
        ),
        compiler_params=pltpu.CompilerParams(vmem_limit_bytes=2 << 20),
    )
    far, near = run(info, planes)
    n = lax.axis_size("seq") * lax.axis_size("fsdp")
    pairs = [(i, i + 1) for i in range(1, n - 1, 2)]
    far = lax.ppermute(far, ("seq", "fsdp"), pairs + [(j, i) for i, j in pairs])
    near = swap_core(near)
    wide = 4 * HEAD_DIM
    run = pl.pallas_call(
        light_kernel,
        out_shape=struct((rows, width)),
        grid=(width // wide,),
        in_specs=[
            SMEM,
            pl.BlockSpec((3, rows, wide), lambda i: (0, 0, i)),
            pl.BlockSpec((2, HALF_WIN, wide), lambda i: (0, 0, i)),
            pl.BlockSpec((2, HALF_WIN, wide), lambda i: (0, 0, i)),
        ],
        out_specs=pl.BlockSpec((rows, wide), lambda i: (0, i)),
        cost_estimate=pl.CostEstimate(
            flops=4 * rows * 2 * rows * width,
            bytes_accessed=12 * rows * width,
            transcendentals=2 * rows * rows * LIGHT_HEADS,
        ),
        compiler_params=pltpu.CompilerParams(vmem_limit_bytes=12 << 20),
    )
    return run(info, planes, far, near)


def heavy_kernel(q_ref, near_ref, far_ref, out_ref):
    rows, width = q_ref.shape
    n = 2 * near_ref.shape[0]
    kv = jnp.concatenate([near_ref[...], far_ref[...]], axis=0)
    first = (iota((8, HEAD_DIM), 1) == 0).astype(BF16)
    marks = lax.dot_general(
        first, kv[:, :HEAD_DIM], (((1,), (1,)), ((), ())), preferred_element_type=F32
    )[0:1]
    lane, row = iota((rows, n), 1), iota((rows, n), 0)
    same = (lax.rem(lane, 2 * CAP) < CAP) == (row < CAP)
    usable = same & (marks < MARK / 2)
    for h in range(width // HEAD_DIM):
        at = slice(h * HEAD_DIM, (h + 1) * HEAD_DIM)
        s = lax.dot_general(
            q_ref[:, at], kv[:, at], (((1,), (1,)), ((), ())), preferred_element_type=F32
        )
        s = jnp.where(usable, s * (1.0 / math.sqrt(HEAD_DIM)), -1e30)
        e = jnp.exp(s - jnp.max(s, axis=1, keepdims=True))
        y = jnp.dot(
            e.astype(BF16),
            kv[:, width + h * HEAD_DIM : width + (h + 1) * HEAD_DIM],
            preferred_element_type=F32,
        )
        out_ref[:, at] = (y / jnp.sum(e, axis=1, keepdims=True)).astype(BF16)


def heavy_branch(qkv, slot_live):
    slots, _, width = qkv.shape
    half = width // 2

    def stacked(x):
        return jnp.concatenate([x[:, :half], x[:, half:]], axis=0)

    q = stacked(qkv[:, 0])
    keys = jnp.where(slot_live[:, None], qkv[:, 1], jnp.bfloat16(MARK))
    kv = jnp.concatenate([stacked(keys), stacked(qkv[:, 2])], axis=1)
    near = jnp.concatenate(gather_seq(kv), axis=0)
    far = swap_core(near)
    out = call(
        heavy_kernel,
        [struct((2 * slots, half))],
        [q, near, far],
        0,
        4 * 2 * slots * 2 * near.shape[0] * half,
    )[0]
    out = jnp.concatenate([out[:slots], out[slots:]], axis=1)
    return jnp.where(slot_live[:, None], out, jnp.bfloat16(0))


def layer(
    tokens, ffn_gain, in_proj, out_proj, router_score, tile_counts, tile_order, light_qkv, heavy_qkv
):
    assert tile_order.shape[1] == 1 and lax.axis_size("fsdp") == 2 and lax.axis_size("dp") == 4
    here = lax.axis_index(("seq", "fsdp")) * tokens.shape[1]
    length = tokens.shape[1] * lax.axis_size("seq") * lax.axis_size("fsdp")
    info = jnp.stack([lax.axis_index("fsdp"), here, jnp.int32(length)]).astype(jnp.int32)
    info, tokens = lax.optimization_barrier((info, tokens))
    core = info
    slot_live = jnp.arange(CAP) < tile_counts[0, 0]
    heavy_ffn, heavy_qkv = routed_ffn(
        core,
        tokens[0],
        ffn_gain[None],
        in_proj,
        out_proj,
        router_score,
        tile_counts,
        tile_order[0],
        heavy_qkv,
    )
    light_out = light_branch(info, jnp.transpose(light_qkv[0], (1, 0, 2)))
    heavy_attn = heavy_branch(heavy_qkv[0], slot_live)
    return (light_out[None], heavy_attn[None], heavy_ffn[None])


def solution(mesh):
    placed = (
        P("dp", ("seq", "fsdp"), None),
        P(),
        P(None, ("dp", "seq", "fsdp")),
        P(("dp", "seq", "fsdp"), None),
        P("dp", ("seq", "fsdp")),
        P("dp", ("seq", "fsdp")),
        P("dp", ("seq", "fsdp"), None),
        P("dp", ("seq", "fsdp"), None, None),
        P("dp", ("seq", "fsdp"), None, None),
    )
    return jax.shard_map(
        layer,
        mesh=mesh,
        in_specs=placed,
        out_specs=(
            P("dp", ("seq", "fsdp"), None),
            P("dp", ("seq", "fsdp"), None),
            P("dp", ("seq", "fsdp"), None),
        ),
        check_vma=False,
    )
```

```python
import functools
import math

import jax
import jax.numpy as jnp
from jax import lax
from jax.experimental import pallas as pl
from jax.experimental.pallas import tpu as pltpu
from jax.sharding import PartitionSpec as P


HEAD_DIM = 128
LIGHT_HEADS = 16
TILE = 128
CAP = 12
MEAN_LIVE = 8
HALF_WIN = 64
MARK = 1048576.0
F32, BF16 = jnp.float32, jnp.bfloat16
VMEM = pl.BlockSpec(memory_space=pltpu.VMEM)
SMEM = pl.BlockSpec(memory_space=pltpu.SMEM)


def iota(shape, dim):
    return lax.broadcasted_iota(jnp.int32, shape, dim)


def call(body, outs, args, scalars, flops, room=4 << 20, **kw):
    size = sum(math.prod(a.shape) * a.dtype.itemsize for a in (*args, *outs))
    return pl.pallas_call(
        body,
        out_shape=outs,
        in_specs=[SMEM] * scalars + [VMEM] * (len(args) - scalars),
        out_specs=[VMEM] * len(outs),
        cost_estimate=pl.CostEstimate(flops=flops, bytes_accessed=size, transcendentals=0),
        compiler_params=pltpu.CompilerParams(vmem_limit_bytes=min(60 << 20, size + room)),
        **kw,
    )(*args)


def struct(shape, dtype=BF16):
    return jax.ShapeDtypeStruct(shape, dtype)


def swap_core(x):
    return lax.ppermute(x, "fsdp", [(0, 1), (1, 0)])


def swap_seq(x, mask):
    n = lax.axis_size("seq")
    return lax.ppermute(x, "seq", [(i, i ^ mask) for i in range(n)])


def swap_doc(x, masks):
    docs = range(lax.axis_size("dp"))
    pairs = [(2 * d + c, 2 * (d ^ masks[c]) + c) for d in docs for c in range(2)]
    return lax.ppermute(x, ("dp", "fsdp"), pairs)


def seq_stages():
    n, stride, out = lax.axis_size("seq"), 1, []
    while stride < n:
        radix = min(4, n // stride)
        out.append((stride, radix))
        stride *= radix
    return out


def gather_seq(x):
    parts = [x]
    for stride, radix in seq_stages():
        x = jnp.concatenate(parts, axis=0) if len(parts) > 1 else parts[0]
        far = {k: swap_seq(x, k * stride) for k in range(radix - 1, 0, -1)}
        parts = [x] + [far[k] for k in range(1, radix)]
    return parts


def scatter_seq(parts):
    stages = seq_stages()
    for at in range(len(stages) - 1, -1, -1):
        stride, radix = stages[at]
        far = {k: swap_seq(parts[k], k * stride) for k in range(radix - 1, 0, -1)}
        total = parts[0].astype(F32)
        for k in range(1, radix):
            total = total + far[k].astype(F32)
        total = total.astype(BF16)
        if at:
            parts = jnp.split(total, stages[at - 1][1], axis=0)
    return total


def pick_kernel(count_ref, tokens_ref, order_ref, gain_ref, out_ref):
    rows, half = out_ref.shape
    slot = lax.rem(iota((rows, 1), 0), CAP)
    lanes = iota((rows, TILE), 1)
    order = jnp.broadcast_to(order_ref[...], (rows, TILE))
    row = jnp.sum(jnp.where(lanes == slot, order, 0), axis=1, keepdims=True)
    x = jnp.dot((lanes == row).astype(BF16), tokens_ref[...], preferred_element_type=F32)
    scale = lax.rsqrt(jnp.mean(x * x, axis=1, keepdims=True) + 1e-06)
    first = iota((rows, 1), 0) < CAP
    x = jnp.where(first, x[:, :half], x[:, half:])
    gain = jnp.where(first, gain_ref[:, :half], gain_ref[:, half:])
    dead = slot >= count_ref[0, 0]
    out_ref[...] = jnp.where(dead, MARK, x * scale * gain).astype(BF16)


def pick_rows(counts, tokens, order, gain):
    rows, width = 2 * CAP, tokens.shape[1]
    return call(
        pick_kernel,
        [struct((rows, width // 2))],
        [counts, tokens, order, gain],
        1,
        2 * rows * TILE * width,
        room=54 << 20,
    )[0]


def compact_kernel(parts, *refs):
    mine, peer, (out_ref, place_ref) = refs[:parts], refs[parts : 2 * parts], refs[2 * parts :]
    live_rows, width = out_ref.shape
    n = mine[0].shape[0]
    core = lax.axis_index("fsdp")
    up, side = iota((n, n), 0), iota((n, n), 1)
    turned = jnp.where(lax.rem(side, 2 * CAP) < CAP, side + CAP, side - CAP)
    own = (lax.rem(iota((n, 1), 0), 2 * CAP) < CAP) == (core == 0)
    usable = (lax.rem(iota((1, n), 1), 2 * CAP) < CAP) == (core == 0)
    base = jnp.zeros((1, 1), F32)
    total = jnp.zeros((live_rows, width), F32)
    for k in range(parts):
        mark = jnp.where(
            own, mine[k][:, 0:128].astype(F32)[:, 0:1], peer[k][:, 0:128].astype(F32)[:, 0:1]
        )
        live = jnp.where(mark < MARK / 2, 1.0, 0.0)
        for ref, at in ((mine[k], side), (peer[k], turned)):
            there = jnp.sum(jnp.where(up == at, live, 0.0), axis=0, keepdims=True)
            ahead = jnp.sum(jnp.where(up < at, live, 0.0), axis=0, keepdims=True) + base
            to_row = iota((live_rows, n), 0).astype(F32) == ahead
            pick = jnp.where(to_row & (there > 0.5) & usable, 1.0, 0.0).astype(BF16)
            total = total + jnp.dot(pick, ref[...], preferred_element_type=F32)
        row = jnp.sum(jnp.where(up == side, live, 0.0), axis=0, keepdims=True)
        ahead = jnp.sum(jnp.where(side < up, row, 0.0), axis=1, keepdims=True) + base
        at = iota((n, live_rows), 1).astype(F32) == ahead
        place_ref[k, :, :] = jnp.where(at & (live > 0.5), 1.0, 0.0).astype(BF16)
        base = base + jnp.sum(live, axis=0, keepdims=True)
    out_ref[...] = total.astype(BF16)


def compact(mine, peer, live_rows):
    n, width = mine[0].shape
    return call(
        functools.partial(compact_kernel, len(mine)),
        [struct((live_rows, width)), struct((len(mine), n, live_rows))],
        [*mine, *peer],
        0,
        4 * len(mine) * n * live_rows * width,
    )


def spread_kernel(parts, terms, place_ref, *refs):
    rows = sum(r[...].astype(F32) for r in refs[:terms]).astype(BF16)
    for k in range(parts):
        refs[terms + k][...] = jnp.dot(
            place_ref[k, :, :], rows, preferred_element_type=F32
        ).astype(BF16)


def spread(place, terms):
    parts, n, live_rows = place.shape
    width = terms[0].shape[1]
    return call(
        functools.partial(spread_kernel, parts, len(terms)),
        [struct((n, width))] * parts,
        [place, *terms],
        0,
        2 * parts * n * live_rows * width,
    )


def ffn_kernel(n, *refs):
    mine, peer, (win_ref, wout_ref) = refs[:n], refs[n : 2 * n], refs[2 * n : 2 * n + 2]
    send, keep = refs[2 * n + 2 : 3 * n + 2], refs[3 * n + 2 :]
    core = lax.axis_index("fsdp")
    rows, half = mine[0].shape
    at_mine = pl.multiple_of(core * half, 128)
    at_peer = pl.multiple_of((1 - core) * half, 128)
    group = max(1, min(n, 256 // rows))
    step = 256
    for first in range(0, n, group):
        roles = range(first, min(n, first + group))
        x_mine = jnp.concatenate([mine[r][...] for r in roles], axis=0)
        x_peer = jnp.concatenate([peer[r][...] for r in roles], axis=0)
        total = jnp.dot(x_mine, win_ref[pl.ds(at_mine, half), :], preferred_element_type=F32)
        total = total + jnp.dot(x_peer, win_ref[pl.ds(at_peer, half), :], preferred_element_type=F32)
        hidden = jnp.maximum(total, 0.0).astype(BF16)

        def columns(i, carry, hidden=hidden, roles=roles):
            off = pl.multiple_of(i * step, step)
            for start, targets in ((at_peer, send), (at_mine, keep)):
                y = jnp.dot(
                    hidden, wout_ref[:, pl.ds(start + off, step)], preferred_element_type=F32
                ).astype(BF16)
                for j, r in enumerate(roles):
                    targets[r][:, pl.ds(off, step)] = y[j * rows : (j + 1) * rows]
            return carry

        lax.fori_loop(0, half // step, columns, 0)


def ffn(mine, peer, win, wout):
    n = len(mine)
    rows, half = mine[0].shape
    outs = call(
        functools.partial(ffn_kernel, n),
        [struct((rows, half))] * (2 * n),
        [*mine, *peer, win, wout],
        0,
        4 * n * rows * 2 * half * win.shape[1],
    )
    return outs[:n], outs[n:]


def finish_kernel(count_ref, mine_ref, peer_ref, order_ref, score_ref, out_ref):
    rows, half = mine_ref.shape
    core = lax.axis_index("fsdp")
    pick = (iota((CAP, rows), 1) == iota((CAP, rows), 0) + core * CAP).astype(BF16)
    lanes, slot = iota((CAP, TILE), 1), iota((CAP, TILE), 0)
    order = jnp.broadcast_to(order_ref[...], (CAP, TILE))
    row = jnp.sum(jnp.where(lanes == slot, order, 0), axis=1, keepdims=True)
    score = jnp.sum(jnp.where(lanes == row, score_ref[...].astype(F32), 0.0), axis=1, keepdims=True)
    score = jnp.where(iota((CAP, 1), 0) < count_ref[0, 0], score, 0.0)
    for ref, start in ((mine_ref, core * half), (peer_ref, (1 - core) * half)):
        y = jnp.dot(pick, ref[...], preferred_element_type=F32)
        out_ref[:, pl.ds(pl.multiple_of(start, 128), half)] = (score * y).astype(BF16)


def finish(counts, mine, peer, order, score):
    rows, half = mine.shape
    return call(
        finish_kernel,
        [struct((CAP, 2 * half))],
        [counts, mine, peer, order, score],
        1,
        4 * CAP * rows * half,
    )[0]


def load_kernel(*refs):
    n = len(refs) // 2
    copies = [pltpu.make_async_copy(refs[i], refs[n + i], refs[2 * n].at[i]) for i in range(n)]
    for c in copies:
        c.start()
    for c in copies:
        c.wait()


def load(*arrays):
    n = len(arrays)
    return pl.pallas_call(
        load_kernel,
        out_shape=[struct(a.shape, a.dtype) for a in arrays],
        in_specs=[pl.BlockSpec(memory_space=pltpu.HBM)] * n,
        out_specs=[VMEM] * n,
        scratch_shapes=[pltpu.SemaphoreType.DMA((n,))],
        cost_estimate=pl.CostEstimate(
            flops=0, bytes_accessed=sum(2 * a.size for a in arrays), transcendentals=0
        ),
        compiler_params=pltpu.CompilerParams(
            vmem_limit_bytes=42 << 20
        ),
    )(*arrays)


def total(*terms):
    return sum(t.astype(F32) for t in terms).astype(BF16)


NEAR, OTHER, DIAGONAL = (2, 1), (1, 2), (3, 3)


def routed_ffn(tokens, gain, win, wout, score, counts, order, heavy_qkv):
    devices = lax.axis_size("seq") * lax.axis_size("fsdp")
    own = pick_rows(counts, tokens, order, gain)
    heavy_qkv, _ = lax.optimization_barrier((heavy_qkv, own))
    win, wout = load(win, wout)
    blocks = gather_seq(own)
    peers = [swap_core(x) for x in blocks]
    x0, place = compact(blocks, peers, MEAN_LIVE * devices)
    x1 = swap_doc(x0, NEAR)
    x2 = swap_doc(x0, OTHER)
    x3 = swap_doc(x1, OTHER)
    p0, p2, p1, p3 = [swap_core(x) for x in (x0, x1, x2, x3)]
    send, keep = ffn((x0, x1, x2), (p0, p1, p2), win, wout)
    back = [swap_core(x) for x in send]
    got1 = swap_doc(total(keep[1], back[2]), NEAR)
    got2 = swap_doc(total(keep[2], back[1]), OTHER)
    send3, keep3 = ffn((x3,), (p3,), win, wout)
    got3 = swap_doc(total(keep3[0], swap_core(send3[0])), DIAGONAL)
    summed = scatter_seq(spread(place, (keep[0], back[0], got1, got2, got3)))
    return finish(counts, summed, swap_core(summed), order, score), heavy_qkv


def light_kernel(qkv_ref, far_ref, near_ref, out_ref):
    rows = qkv_ref.shape[1]
    core = lax.axis_index("fsdp")
    first_pos = lax.axis_index(("seq", "fsdp")) * rows
    length = rows * lax.axis_size("seq") * lax.axis_size("fsdp")
    span = rows + 2 * HALF_WIN
    lane = iota((rows, span), 1)
    row = iota((rows, span), 0)
    turn = jnp.where(core == 0, 0, rows + HALF_WIN)
    col = jnp.where(
        lane < HALF_WIN,
        lane + turn,
        jnp.where(lane < HALF_WIN + rows, lane, lane - turn),
    )
    pos = first_pos - HALF_WIN + col
    inside = (col >= row) & (col < row + 2 * HALF_WIN) & (pos >= 0) & (pos < length)
    bias = jnp.where(inside, 0.0, -1e30)
    for h in range(out_ref.shape[1] // HEAD_DIM):
        at = slice(h * HEAD_DIM, (h + 1) * HEAD_DIM)
        keys = jnp.concatenate([far_ref[0, :, at], qkv_ref[1, :, at], near_ref[0, :, at]], axis=0)
        values = jnp.concatenate([far_ref[1, :, at], qkv_ref[2, :, at], near_ref[1, :, at]], axis=0)
        s = lax.dot_general(
            qkv_ref[0, :, at], keys, (((1,), (1,)), ((), ())), preferred_element_type=F32
        )
        s = s * (1.0 / math.sqrt(HEAD_DIM)) + bias
        e = jnp.exp(s - jnp.max(s, axis=1, keepdims=True))
        y = jnp.dot(e.astype(BF16), values, preferred_element_type=F32)
        out_ref[:, at] = (y / jnp.sum(e, axis=1, keepdims=True)).astype(BF16)


def halo_kernel(planes_ref, far_ref, near_ref, sems):
    last = planes_ref.shape[1] - HALF_WIN
    edge = pl.multiple_of(lax.axis_index("fsdp") * last, HALF_WIN)
    other = pl.multiple_of(last - edge, HALF_WIN)
    copies = [
        pltpu.make_async_copy(planes_ref.at[1:3, pl.ds(at, HALF_WIN)], ref, sems.at[i])
        for i, (at, ref) in enumerate(((edge, far_ref), (other, near_ref)))
    ]
    for c in copies:
        c.start()
    for c in copies:
        c.wait()


def light_branch(planes):
    _, rows, width = planes.shape
    run = pl.pallas_call(
        halo_kernel,
        out_shape=[struct((2, HALF_WIN, width))] * 2,
        in_specs=[pl.BlockSpec(memory_space=pl.ANY)],
        out_specs=[VMEM] * 2,
        scratch_shapes=[pltpu.SemaphoreType.DMA((2,))],
        cost_estimate=pl.CostEstimate(
            flops=0, bytes_accessed=8 * HALF_WIN * width, transcendentals=0
        ),
        compiler_params=pltpu.CompilerParams(vmem_limit_bytes=48 << 20),
    )
    far, near = run(planes)
    n = lax.axis_size("seq") * lax.axis_size("fsdp")
    pairs = [(i, i + 1) for i in range(1, n - 1, 2)]
    far = lax.ppermute(far, ("seq", "fsdp"), pairs + [(j, i) for i, j in pairs])
    near = swap_core(near)
    wide = 4 * HEAD_DIM
    run = pl.pallas_call(
        light_kernel,
        out_shape=struct((rows, width)),
        grid=(width // wide,),
        in_specs=[
            pl.BlockSpec((3, rows, wide), lambda i: (0, 0, i)),
            pl.BlockSpec((2, HALF_WIN, wide), lambda i: (0, 0, i)),
            pl.BlockSpec((2, HALF_WIN, wide), lambda i: (0, 0, i)),
        ],
        out_specs=pl.BlockSpec((rows, wide), lambda i: (0, i)),
        cost_estimate=pl.CostEstimate(
            flops=4 * rows * 2 * rows * width,
            bytes_accessed=12 * rows * width,
            transcendentals=2 * rows * rows * LIGHT_HEADS,
        ),
        compiler_params=pltpu.CompilerParams(vmem_limit_bytes=12 << 20),
    )
    return run(planes, far, near)


def heavy_kernel(q_ref, near_ref, far_ref, out_ref):
    rows, width = q_ref.shape
    n = 2 * near_ref.shape[0]
    kv = jnp.concatenate([near_ref[...], far_ref[...]], axis=0)
    first = (iota((8, HEAD_DIM), 1) == 0).astype(BF16)
    marks = lax.dot_general(
        first, kv[:, :HEAD_DIM], (((1,), (1,)), ((), ())), preferred_element_type=F32
    )[0:1]
    lane, row = iota((rows, n), 1), iota((rows, n), 0)
    same = (lax.rem(lane, 2 * CAP) < CAP) == (row < CAP)
    usable = same & (marks < MARK / 2)
    for h in range(width // HEAD_DIM):
        at = slice(h * HEAD_DIM, (h + 1) * HEAD_DIM)
        s = lax.dot_general(
            q_ref[:, at], kv[:, at], (((1,), (1,)), ((), ())), preferred_element_type=F32
        )
        s = jnp.where(usable, s * (1.0 / math.sqrt(HEAD_DIM)), -1e30)
        e = jnp.exp(s - jnp.max(s, axis=1, keepdims=True))
        y = jnp.dot(
            e.astype(BF16),
            kv[:, width + h * HEAD_DIM : width + (h + 1) * HEAD_DIM],
            preferred_element_type=F32,
        )
        out_ref[:, at] = (y / jnp.sum(e, axis=1, keepdims=True)).astype(BF16)


def heavy_branch(qkv, slot_live):
    slots, _, width = qkv.shape
    half = width // 2

    def stacked(x):
        return jnp.concatenate([x[:, :half], x[:, half:]], axis=0)

    q = stacked(qkv[:, 0])
    keys = jnp.where(slot_live[:, None], qkv[:, 1], jnp.bfloat16(MARK))
    kv = jnp.concatenate([stacked(keys), stacked(qkv[:, 2])], axis=1)
    near = jnp.concatenate(gather_seq(kv), axis=0)
    far = swap_core(near)
    out = call(
        heavy_kernel,
        [struct((2 * slots, half))],
        [q, near, far],
        0,
        4 * 2 * slots * 2 * near.shape[0] * half,
    )[0]
    out = jnp.concatenate([out[:slots], out[slots:]], axis=1)
    return jnp.where(slot_live[:, None], out, jnp.bfloat16(0))


def layer(
    tokens, ffn_gain, in_proj, out_proj, router_score, tile_counts, tile_order, light_qkv, heavy_qkv
):
    assert tile_order.shape[1] == 1 and lax.axis_size("fsdp") == 2 and lax.axis_size("dp") == 4
    slot_live = jnp.arange(CAP) < tile_counts[0, 0]
    heavy_ffn, heavy_qkv = routed_ffn(
        tokens[0],
        ffn_gain[None],
        in_proj,
        out_proj,
        router_score,
        tile_counts,
        tile_order[0],
        heavy_qkv,
    )
    light_out = light_branch(jnp.transpose(light_qkv[0], (1, 0, 2)))
    heavy_attn = heavy_branch(heavy_qkv[0], slot_live)
    return (light_out[None], heavy_attn[None], heavy_ffn[None])


def solution(mesh):
    placed = (
        P("dp", ("seq", "fsdp"), None),
        P(),
        P(None, ("dp", "seq", "fsdp")),
        P(("dp", "seq", "fsdp"), None),
        P("dp", ("seq", "fsdp")),
        P("dp", ("seq", "fsdp")),
        P("dp", ("seq", "fsdp"), None),
        P("dp", ("seq", "fsdp"), None, None),
        P("dp", ("seq", "fsdp"), None, None),
    )
    return jax.shard_map(
        layer,
        mesh=mesh,
        in_specs=placed,
        out_specs=(
            P("dp", ("seq", "fsdp"), None),
            P("dp", ("seq", "fsdp"), None),
            P("dp", ("seq", "fsdp"), None),
        ),
        check_vma=False,
    )
```

```python
import functools
import math

import jax
import jax.numpy as jnp
from jax import lax
from jax.experimental import pallas as pl
from jax.experimental.pallas import tpu as pltpu
from jax.sharding import PartitionSpec as P


HEAD_DIM = 128
LIGHT_HEADS = 16
TILE = 128
CAP = 12
MEAN_LIVE = 8
HALF_WIN = 64
MARK = 1048576.0
F32, BF16 = jnp.float32, jnp.bfloat16
VMEM = pl.BlockSpec(memory_space=pltpu.VMEM)
SMEM = pl.BlockSpec(memory_space=pltpu.SMEM)


def iota(shape, dim):
    return lax.broadcasted_iota(jnp.int32, shape, dim)


def call(body, outs, args, scalars, flops, room=4 << 20, **kw):
    size = sum(math.prod(a.shape) * a.dtype.itemsize for a in (*args, *outs))
    return pl.pallas_call(
        body,
        out_shape=outs,
        in_specs=[SMEM] * scalars + [VMEM] * (len(args) - scalars),
        out_specs=[VMEM] * len(outs),
        cost_estimate=pl.CostEstimate(flops=flops, bytes_accessed=size, transcendentals=0),
        compiler_params=pltpu.CompilerParams(vmem_limit_bytes=min(60 << 20, size + room)),
        **kw,
    )(*args)


def struct(shape, dtype=BF16):
    return jax.ShapeDtypeStruct(shape, dtype)


def swap_core(x):
    return lax.ppermute(x, "fsdp", [(0, 1), (1, 0)])


def swap_seq(x, mask):
    n = lax.axis_size("seq")
    return lax.ppermute(x, "seq", [(i, i ^ mask) for i in range(n)])


def swap_doc(x, masks):
    docs = range(lax.axis_size("dp"))
    pairs = [(2 * d + c, 2 * (d ^ masks[c]) + c) for d in docs for c in range(2)]
    return lax.ppermute(x, ("dp", "fsdp"), pairs)


def seq_stages():
    n, stride, out = lax.axis_size("seq"), 1, []
    while stride < n:
        radix = min(4, n // stride)
        out.append((stride, radix))
        stride *= radix
    return out


def gather_seq(x):
    parts = [x]
    for stride, radix in seq_stages():
        x = jnp.concatenate(parts, axis=0) if len(parts) > 1 else parts[0]
        far = {k: swap_seq(x, k * stride) for k in range(radix - 1, 0, -1)}
        parts = [x] + [far[k] for k in range(1, radix)]
    return parts


def scatter_seq(parts):
    stages = seq_stages()
    for at in range(len(stages) - 1, -1, -1):
        stride, radix = stages[at]
        far = {k: swap_seq(parts[k], k * stride) for k in range(radix - 1, 0, -1)}
        total = parts[0].astype(F32)
        for k in range(1, radix):
            total = total + far[k].astype(F32)
        total = total.astype(BF16)
        if at:
            parts = jnp.split(total, stages[at - 1][1], axis=0)
    return total


def pick_kernel(count_ref, tokens_ref, order_ref, gain_ref, out_ref):
    rows, half = out_ref.shape
    slot = lax.rem(iota((rows, 1), 0), CAP)
    lanes = iota((rows, TILE), 1)
    order = jnp.broadcast_to(order_ref[...], (rows, TILE))
    row = jnp.sum(jnp.where(lanes == slot, order, 0), axis=1, keepdims=True)
    x = jnp.dot((lanes == row).astype(BF16), tokens_ref[...], preferred_element_type=F32)
    scale = lax.rsqrt(jnp.mean(x * x, axis=1, keepdims=True) + 1e-06)
    first = iota((rows, 1), 0) < CAP
    x = jnp.where(first, x[:, :half], x[:, half:])
    gain = jnp.where(first, gain_ref[:, :half], gain_ref[:, half:])
    dead = slot >= count_ref[0, 0]
    out_ref[...] = jnp.where(dead, MARK, x * scale * gain).astype(BF16)


def pick_rows(counts, tokens, order, gain):
    rows, width = 2 * CAP, tokens.shape[1]
    return call(
        pick_kernel,
        [struct((rows, width // 2))],
        [counts, tokens, order, gain],
        1,
        2 * rows * TILE * width,
        room=54 << 20,
    )[0]


def compact_kernel(parts, *refs):
    mine, peer, (out_ref, place_ref) = refs[:parts], refs[parts : 2 * parts], refs[2 * parts :]
    live_rows, width = out_ref.shape
    n = mine[0].shape[0]
    core = lax.axis_index("fsdp")
    up, side = iota((n, n), 0), iota((n, n), 1)
    turned = jnp.where(lax.rem(side, 2 * CAP) < CAP, side + CAP, side - CAP)
    own = (lax.rem(iota((n, 1), 0), 2 * CAP) < CAP) == (core == 0)
    usable = (lax.rem(iota((1, n), 1), 2 * CAP) < CAP) == (core == 0)
    base = jnp.zeros((1, 1), F32)
    total = jnp.zeros((live_rows, width), F32)
    for k in range(parts):
        mark = jnp.where(
            own, mine[k][:, 0:128].astype(F32)[:, 0:1], peer[k][:, 0:128].astype(F32)[:, 0:1]
        )
        live = jnp.where(mark < MARK / 2, 1.0, 0.0)
        for ref, at in ((mine[k], side), (peer[k], turned)):
            there = jnp.sum(jnp.where(up == at, live, 0.0), axis=0, keepdims=True)
            ahead = jnp.sum(jnp.where(up < at, live, 0.0), axis=0, keepdims=True) + base
            to_row = iota((live_rows, n), 0).astype(F32) == ahead
            pick = jnp.where(to_row & (there > 0.5) & usable, 1.0, 0.0).astype(BF16)
            total = total + jnp.dot(pick, ref[...], preferred_element_type=F32)
        row = jnp.sum(jnp.where(up == side, live, 0.0), axis=0, keepdims=True)
        ahead = jnp.sum(jnp.where(side < up, row, 0.0), axis=1, keepdims=True) + base
        at = iota((n, live_rows), 1).astype(F32) == ahead
        place_ref[k, :, :] = jnp.where(at & (live > 0.5), 1.0, 0.0).astype(BF16)
        base = base + jnp.sum(live, axis=0, keepdims=True)
    out_ref[...] = total.astype(BF16)


def compact(mine, peer, live_rows):
    n, width = mine[0].shape
    return call(
        functools.partial(compact_kernel, len(mine)),
        [struct((live_rows, width)), struct((len(mine), n, live_rows))],
        [*mine, *peer],
        0,
        4 * len(mine) * n * live_rows * width,
    )


def spread_kernel(parts, terms, place_ref, *refs):
    rows = sum(r[...].astype(F32) for r in refs[:terms]).astype(BF16)
    for k in range(parts):
        refs[terms + k][...] = jnp.dot(
            place_ref[k, :, :], rows, preferred_element_type=F32
        ).astype(BF16)


def spread(place, terms):
    parts, n, live_rows = place.shape
    width = terms[0].shape[1]
    return call(
        functools.partial(spread_kernel, parts, len(terms)),
        [struct((n, width))] * parts,
        [place, *terms],
        0,
        2 * parts * n * live_rows * width,
    )


def enter_kernel(*refs):
    *rows, win_ref, out_ref = refs
    half = rows[0].shape[1]
    at = pl.multiple_of(lax.axis_index("fsdp") * half, 128)
    group = max(1, 256 // rows[0].shape[0])
    for first in range(0, len(rows), group):
        x = jnp.concatenate([r[...] for r in rows[first : first + group]], axis=0)
        at_row = first * rows[0].shape[0]
        out_ref[at_row : at_row + x.shape[0], :] = jnp.dot(
            x, win_ref[pl.ds(at, half), :], preferred_element_type=F32
        )


def enter(rows, win):
    count, half = rows[0].shape
    return call(
        enter_kernel,
        [struct((len(rows) * count, win.shape[1]), F32)],
        [*rows, win],
        0,
        2 * len(rows) * count * half * win.shape[1],
    )[0]


def leave_kernel(n, *refs):
    part_ref, peer, (win_ref, wout_ref) = refs[0], refs[1 : n + 1], refs[n + 1 : n + 3]
    send, keep = refs[n + 3 : 2 * n + 3], refs[2 * n + 3 :]
    core = lax.axis_index("fsdp")
    rows, half = peer[0].shape
    at_mine = pl.multiple_of(core * half, 128)
    at_peer = pl.multiple_of((1 - core) * half, 128)
    group = max(1, min(n, 256 // rows))
    step = half
    for first in range(0, n, group):
        roles = range(first, min(n, first + group))
        x = jnp.concatenate([peer[r][...] for r in roles], axis=0)
        total = part_ref[first * rows : first * rows + x.shape[0], :] + jnp.dot(
            x, win_ref[pl.ds(at_peer, half), :], preferred_element_type=F32
        )
        hidden = jnp.maximum(total, 0.0).astype(BF16)

        def columns(i, carry, hidden=hidden, roles=roles):
            off = pl.multiple_of(i * step, step)
            for start, targets in ((at_peer, send), (at_mine, keep)):
                y = jnp.dot(
                    hidden, wout_ref[:, pl.ds(start + off, step)], preferred_element_type=F32
                ).astype(BF16)
                for j, r in enumerate(roles):
                    targets[r][:, pl.ds(off, step)] = y[j * rows : (j + 1) * rows]
            return carry

        lax.fori_loop(0, half // step, columns, 0)


def leave(part, peer, win, wout):
    n = len(peer)
    rows, half = peer[0].shape
    outs = call(
        functools.partial(leave_kernel, n),
        [struct((rows, half))] * (2 * n),
        [part, *peer, win, wout],
        0,
        6 * n * rows * half * win.shape[1],
    )
    return outs[:n], outs[n:]


def finish_kernel(count_ref, mine_ref, peer_ref, order_ref, score_ref, out_ref):
    rows, half = mine_ref.shape
    core = lax.axis_index("fsdp")
    pick = (iota((CAP, rows), 1) == iota((CAP, rows), 0) + core * CAP).astype(BF16)
    lanes, slot = iota((CAP, TILE), 1), iota((CAP, TILE), 0)
    order = jnp.broadcast_to(order_ref[...], (CAP, TILE))
    row = jnp.sum(jnp.where(lanes == slot, order, 0), axis=1, keepdims=True)
    score = jnp.sum(jnp.where(lanes == row, score_ref[...].astype(F32), 0.0), axis=1, keepdims=True)
    score = jnp.where(iota((CAP, 1), 0) < count_ref[0, 0], score, 0.0)
    for ref, start in ((mine_ref, core * half), (peer_ref, (1 - core) * half)):
        y = jnp.dot(pick, ref[...], preferred_element_type=F32)
        out_ref[:, pl.ds(pl.multiple_of(start, 128), half)] = (score * y).astype(BF16)


def finish(counts, mine, peer, order, score):
    rows, half = mine.shape
    return call(
        finish_kernel,
        [struct((CAP, 2 * half))],
        [counts, mine, peer, order, score],
        1,
        4 * CAP * rows * half,
    )[0]


def load_kernel(*refs):
    n = len(refs) // 2
    copies = [pltpu.make_async_copy(refs[i], refs[n + i], refs[2 * n].at[i]) for i in range(n)]
    for c in copies:
        c.start()
    for c in copies:
        c.wait()


def load(*arrays):
    n = len(arrays)
    return pl.pallas_call(
        load_kernel,
        out_shape=[struct(a.shape, a.dtype) for a in arrays],
        in_specs=[pl.BlockSpec(memory_space=pltpu.HBM)] * n,
        out_specs=[VMEM] * n,
        scratch_shapes=[pltpu.SemaphoreType.DMA((n,))],
        cost_estimate=pl.CostEstimate(
            flops=0, bytes_accessed=sum(2 * a.size for a in arrays), transcendentals=0
        ),
        compiler_params=pltpu.CompilerParams(
            vmem_limit_bytes=42 << 20
        ),
    )(*arrays)


def total(*terms):
    return sum(t.astype(F32) for t in terms).astype(BF16)


NEAR, OTHER, DIAGONAL = (2, 1), (1, 2), (3, 3)


def routed_ffn(tokens, gain, win, wout, score, counts, order, heavy_qkv):
    devices = lax.axis_size("seq") * lax.axis_size("fsdp")
    own = pick_rows(counts, tokens, order, gain)
    win, wout = load(win, wout)
    blocks = gather_seq(own)
    peers = [swap_core(x) for x in blocks]
    x0, place = compact(blocks, peers, MEAN_LIVE * devices)
    heavy_qkv, _ = lax.optimization_barrier((heavy_qkv, x0))
    x1 = swap_doc(x0, NEAR)
    x2 = swap_doc(x0, OTHER)
    x3 = swap_doc(x1, OTHER)
    p0, p2, p1, p3 = [swap_core(x) for x in (x0, x1, x2, x3)]
    send, keep = leave(enter((x0, x1, x2), win), (p0, p1, p2), win, wout)
    back = [swap_core(x) for x in send]
    got1 = swap_doc(total(keep[1], back[2]), NEAR)
    got2 = swap_doc(total(keep[2], back[1]), OTHER)
    send3, keep3 = leave(enter((x3,), win), (p3,), win, wout)
    got3 = swap_doc(total(keep3[0], swap_core(send3[0])), DIAGONAL)
    summed = scatter_seq(spread(place, (keep[0], back[0], got1, got2, got3)))
    return finish(counts, summed, swap_core(summed), order, score), heavy_qkv


def light_kernel(qkv_ref, far_ref, near_ref, out_ref):
    rows = qkv_ref.shape[1]
    core = lax.axis_index("fsdp")
    first_pos = lax.axis_index(("seq", "fsdp")) * rows
    length = rows * lax.axis_size("seq") * lax.axis_size("fsdp")
    span = rows + 2 * HALF_WIN
    lane = iota((rows, span), 1)
    row = iota((rows, span), 0)
    turn = jnp.where(core == 0, 0, rows + HALF_WIN)
    col = jnp.where(
        lane < HALF_WIN,
        lane + turn,
        jnp.where(lane < HALF_WIN + rows, lane, lane - turn),
    )
    pos = first_pos - HALF_WIN + col
    inside = (col >= row) & (col < row + 2 * HALF_WIN) & (pos >= 0) & (pos < length)
    bias = jnp.where(inside, 0.0, -1e30)
    for h in range(out_ref.shape[1] // HEAD_DIM):
        at = slice(h * HEAD_DIM, (h + 1) * HEAD_DIM)
        keys = jnp.concatenate([far_ref[0, :, at], qkv_ref[1, :, at], near_ref[0, :, at]], axis=0)
        values = jnp.concatenate([far_ref[1, :, at], qkv_ref[2, :, at], near_ref[1, :, at]], axis=0)
        s = lax.dot_general(
            qkv_ref[0, :, at], keys, (((1,), (1,)), ((), ())), preferred_element_type=F32
        )
        s = s * (1.0 / math.sqrt(HEAD_DIM)) + bias
        e = jnp.exp(s - jnp.max(s, axis=1, keepdims=True))
        y = jnp.dot(e.astype(BF16), values, preferred_element_type=F32)
        out_ref[:, at] = (y / jnp.sum(e, axis=1, keepdims=True)).astype(BF16)


def halo_kernel(planes_ref, far_ref, near_ref, sems):
    last = planes_ref.shape[1] - HALF_WIN
    edge = pl.multiple_of(lax.axis_index("fsdp") * last, HALF_WIN)
    other = pl.multiple_of(last - edge, HALF_WIN)
    copies = [
        pltpu.make_async_copy(planes_ref.at[1:3, pl.ds(at, HALF_WIN)], ref, sems.at[i])
        for i, (at, ref) in enumerate(((edge, far_ref), (other, near_ref)))
    ]
    for c in copies:
        c.start()
    for c in copies:
        c.wait()


def light_branch(planes):
    _, rows, width = planes.shape
    run = pl.pallas_call(
        halo_kernel,
        out_shape=[struct((2, HALF_WIN, width))] * 2,
        in_specs=[pl.BlockSpec(memory_space=pl.ANY)],
        out_specs=[VMEM] * 2,
        scratch_shapes=[pltpu.SemaphoreType.DMA((2,))],
        cost_estimate=pl.CostEstimate(
            flops=0, bytes_accessed=8 * HALF_WIN * width, transcendentals=0
        ),
        compiler_params=pltpu.CompilerParams(vmem_limit_bytes=48 << 20),
    )
    far, near = run(planes)
    n = lax.axis_size("seq") * lax.axis_size("fsdp")
    pairs = [(i, i + 1) for i in range(1, n - 1, 2)]
    far = lax.ppermute(far, ("seq", "fsdp"), pairs + [(j, i) for i, j in pairs])
    near = swap_core(near)
    wide = 4 * HEAD_DIM
    run = pl.pallas_call(
        light_kernel,
        out_shape=struct((rows, width)),
        grid=(width // wide,),
        in_specs=[
            pl.BlockSpec((3, rows, wide), lambda i: (0, 0, i)),
            pl.BlockSpec((2, HALF_WIN, wide), lambda i: (0, 0, i)),
            pl.BlockSpec((2, HALF_WIN, wide), lambda i: (0, 0, i)),
        ],
        out_specs=pl.BlockSpec((rows, wide), lambda i: (0, i)),
        cost_estimate=pl.CostEstimate(
            flops=4 * rows * 2 * rows * width,
            bytes_accessed=12 * rows * width,
            transcendentals=2 * rows * rows * LIGHT_HEADS,
        ),
        compiler_params=pltpu.CompilerParams(vmem_limit_bytes=12 << 20),
    )
    return run(planes, far, near)


def heavy_kernel(q_ref, near_ref, far_ref, out_ref):
    rows, width = q_ref.shape
    n = 2 * near_ref.shape[0]
    kv = jnp.concatenate([near_ref[...], far_ref[...]], axis=0)
    first = (iota((8, HEAD_DIM), 1) == 0).astype(BF16)
    marks = lax.dot_general(
        first, kv[:, :HEAD_DIM], (((1,), (1,)), ((), ())), preferred_element_type=F32
    )[0:1]
    lane, row = iota((rows, n), 1), iota((rows, n), 0)
    same = (lax.rem(lane, 2 * CAP) < CAP) == (row < CAP)
    usable = same & (marks < MARK / 2)
    for h in range(width // HEAD_DIM):
        at = slice(h * HEAD_DIM, (h + 1) * HEAD_DIM)
        s = lax.dot_general(
            q_ref[:, at], kv[:, at], (((1,), (1,)), ((), ())), preferred_element_type=F32
        )
        s = jnp.where(usable, s * (1.0 / math.sqrt(HEAD_DIM)), -1e30)
        e = jnp.exp(s - jnp.max(s, axis=1, keepdims=True))
        y = jnp.dot(
            e.astype(BF16),
            kv[:, width + h * HEAD_DIM : width + (h + 1) * HEAD_DIM],
            preferred_element_type=F32,
        )
        out_ref[:, at] = (y / jnp.sum(e, axis=1, keepdims=True)).astype(BF16)


def heavy_branch(qkv, slot_live):
    slots, _, width = qkv.shape
    half = width // 2

    def stacked(x):
        return jnp.concatenate([x[:, :half], x[:, half:]], axis=0)

    q = stacked(qkv[:, 0])
    keys = jnp.where(slot_live[:, None], qkv[:, 1], jnp.bfloat16(MARK))
    kv = jnp.concatenate([stacked(keys), stacked(qkv[:, 2])], axis=1)
    parts = gather_seq(kv)
    near = jnp.concatenate(parts, axis=0)
    far = swap_core(near)
    out = call(
        heavy_kernel,
        [struct((2 * slots, half))],
        [q, near, far],
        0,
        4 * 2 * slots * 2 * near.shape[0] * half,
    )[0]
    out = jnp.concatenate([out[:slots], out[slots:]], axis=1)
    return jnp.where(slot_live[:, None], out, jnp.bfloat16(0))


def layer(
    tokens, ffn_gain, in_proj, out_proj, router_score, tile_counts, tile_order, light_qkv, heavy_qkv
):
    assert tile_order.shape[1] == 1 and lax.axis_size("fsdp") == 2 and lax.axis_size("dp") == 4
    slot_live = jnp.arange(CAP) < tile_counts[0, 0]
    heavy_ffn, heavy_qkv = routed_ffn(
        tokens[0],
        ffn_gain[None],
        in_proj,
        out_proj,
        router_score,
        tile_counts,
        tile_order[0],
        heavy_qkv,
    )
    light_out = light_branch(jnp.transpose(light_qkv[0], (1, 0, 2)))
    heavy_attn = heavy_branch(heavy_qkv[0], slot_live)
    return (light_out[None], heavy_attn[None], heavy_ffn[None])


def solution(mesh):
    placed = (
        P("dp", ("seq", "fsdp"), None),
        P(),
        P(None, ("dp", "seq", "fsdp")),
        P(("dp", "seq", "fsdp"), None),
        P("dp", ("seq", "fsdp")),
        P("dp", ("seq", "fsdp")),
        P("dp", ("seq", "fsdp"), None),
        P("dp", ("seq", "fsdp"), None, None),
        P("dp", ("seq", "fsdp"), None, None),
    )
    return jax.shard_map(
        layer,
        mesh=mesh,
        in_specs=placed,
        out_specs=(
            P("dp", ("seq", "fsdp"), None),
            P("dp", ("seq", "fsdp"), None),
            P("dp", ("seq", "fsdp"), None),
        ),
        check_vma=False,
    )
```

```python
import functools
import math

import jax
import jax.numpy as jnp
from jax import lax
from jax.experimental import pallas as pl
from jax.experimental.pallas import tpu as pltpu
from jax.sharding import PartitionSpec as P


HEAD_DIM = 128
LIGHT_HEADS = 16
TILE = 128
CAP = 12
MEAN_LIVE = 8
HALF_WIN = 64
MARK = 1048576.0
F32, BF16 = jnp.float32, jnp.bfloat16
VMEM = pl.BlockSpec(memory_space=pltpu.VMEM)
SMEM = pl.BlockSpec(memory_space=pltpu.SMEM)


def iota(shape, dim):
    return lax.broadcasted_iota(jnp.int32, shape, dim)


def call(body, outs, args, scalars, flops, room=4 << 20, **kw):
    size = sum(math.prod(a.shape) * a.dtype.itemsize for a in (*args, *outs))
    return pl.pallas_call(
        body,
        out_shape=outs,
        in_specs=[SMEM] * scalars + [VMEM] * (len(args) - scalars),
        out_specs=[VMEM] * len(outs),
        cost_estimate=pl.CostEstimate(flops=flops, bytes_accessed=size, transcendentals=0),
        compiler_params=pltpu.CompilerParams(vmem_limit_bytes=min(60 << 20, size + room)),
        **kw,
    )(*args)


def struct(shape, dtype=BF16):
    return jax.ShapeDtypeStruct(shape, dtype)


def swap_core(x):
    return lax.ppermute(x, "fsdp", [(0, 1), (1, 0)])


def swap_seq(x, mask):
    n = lax.axis_size("seq")
    return lax.ppermute(x, "seq", [(i, i ^ mask) for i in range(n)])


def swap_doc(x, masks):
    docs = range(lax.axis_size("dp"))
    pairs = [(2 * d + c, 2 * (d ^ masks[c]) + c) for d in docs for c in range(2)]
    return lax.ppermute(x, ("dp", "fsdp"), pairs)


def seq_stages():
    n, stride, out = lax.axis_size("seq"), 1, []
    while stride < n:
        radix = min(4, n // stride)
        out.append((stride, radix))
        stride *= radix
    return out


def gather_seq(x):
    parts = [x]
    for stride, radix in seq_stages():
        x = jnp.concatenate(parts, axis=0) if len(parts) > 1 else parts[0]
        far = {k: swap_seq(x, k * stride) for k in range(radix - 1, 0, -1)}
        parts = [x] + [far[k] for k in range(1, radix)]
    return parts


def scatter_seq(parts):
    stages = seq_stages()
    for at in range(len(stages) - 1, -1, -1):
        stride, radix = stages[at]
        far = {k: swap_seq(parts[k], k * stride) for k in range(radix - 1, 0, -1)}
        total = parts[0].astype(F32)
        for k in range(1, radix):
            total = total + far[k].astype(F32)
        total = total.astype(BF16)
        if at:
            parts = jnp.split(total, stages[at - 1][1], axis=0)
    return total


def pick_kernel(count_ref, tokens_ref, order_ref, gain_ref, out_ref):
    rows, half = out_ref.shape
    slot = lax.rem(iota((rows, 1), 0), CAP)
    lanes = iota((rows, TILE), 1)
    order = jnp.broadcast_to(order_ref[...], (rows, TILE))
    row = jnp.sum(jnp.where(lanes == slot, order, 0), axis=1, keepdims=True)
    x = jnp.dot((lanes == row).astype(BF16), tokens_ref[...], preferred_element_type=F32)
    scale = lax.rsqrt(jnp.mean(x * x, axis=1, keepdims=True) + 1e-06)
    first = iota((rows, 1), 0) < CAP
    x = jnp.where(first, x[:, :half], x[:, half:])
    gain = jnp.where(first, gain_ref[:, :half], gain_ref[:, half:])
    dead = slot >= count_ref[...]
    out_ref[...] = jnp.where(dead, MARK, x * scale * gain).astype(BF16)


def pick_rows(counts, tokens, order, gain):
    rows, width = 2 * CAP, tokens.shape[1]
    return call(
        pick_kernel,
        [struct((rows, width // 2))],
        [counts, tokens, order, gain],
        0,
        2 * rows * TILE * width,
        room=54 << 20,
    )[0]


def compact_kernel(parts, *refs):
    mine, peer, (out_ref, place_ref) = refs[:parts], refs[parts : 2 * parts], refs[2 * parts :]
    live_rows, width = out_ref.shape
    n = mine[0].shape[0]
    core = lax.axis_index("fsdp")
    up, side = iota((n, n), 0), iota((n, n), 1)
    turned = jnp.where(lax.rem(side, 2 * CAP) < CAP, side + CAP, side - CAP)
    own = (lax.rem(iota((n, 1), 0), 2 * CAP) < CAP) == (core == 0)
    usable = (lax.rem(iota((1, n), 1), 2 * CAP) < CAP) == (core == 0)
    base = jnp.zeros((1, 1), F32)
    total = jnp.zeros((live_rows, width), F32)
    for k in range(parts):
        mark = jnp.where(
            own, mine[k][:, 0:128].astype(F32)[:, 0:1], peer[k][:, 0:128].astype(F32)[:, 0:1]
        )
        live = jnp.where(mark < MARK / 2, 1.0, 0.0)
        for ref, at in ((mine[k], side), (peer[k], turned)):
            there = jnp.sum(jnp.where(up == at, live, 0.0), axis=0, keepdims=True)
            ahead = jnp.sum(jnp.where(up < at, live, 0.0), axis=0, keepdims=True) + base
            to_row = iota((live_rows, n), 0).astype(F32) == ahead
            pick = jnp.where(to_row & (there > 0.5) & usable, 1.0, 0.0).astype(BF16)
            total = total + jnp.dot(pick, ref[...], preferred_element_type=F32)
        row = jnp.sum(jnp.where(up == side, live, 0.0), axis=0, keepdims=True)
        ahead = jnp.sum(jnp.where(side < up, row, 0.0), axis=1, keepdims=True) + base
        at = iota((n, live_rows), 1).astype(F32) == ahead
        place_ref[k, :, :] = jnp.where(at & (live > 0.5), 1.0, 0.0).astype(BF16)
        base = base + jnp.sum(live, axis=0, keepdims=True)
    out_ref[...] = total.astype(BF16)


def compact(mine, peer, live_rows):
    n, width = mine[0].shape
    return call(
        functools.partial(compact_kernel, len(mine)),
        [struct((live_rows, width)), struct((len(mine), n, live_rows))],
        [*mine, *peer],
        0,
        4 * len(mine) * n * live_rows * width,
    )


def spread_kernel(parts, terms, place_ref, *refs):
    rows = sum(r[...].astype(F32) for r in refs[:terms]).astype(BF16)
    for k in range(parts):
        refs[terms + k][...] = jnp.dot(
            place_ref[k, :, :], rows, preferred_element_type=F32
        ).astype(BF16)


def spread(place, terms):
    parts, n, live_rows = place.shape
    width = terms[0].shape[1]
    return call(
        functools.partial(spread_kernel, parts, len(terms)),
        [struct((n, width))] * parts,
        [place, *terms],
        0,
        2 * parts * n * live_rows * width,
    )


def enter_kernel(*refs):
    *rows, win_ref, out_ref = refs
    half = rows[0].shape[1]
    at = pl.multiple_of(lax.axis_index("fsdp") * half, 128)
    group = max(1, 256 // rows[0].shape[0])
    for first in range(0, len(rows), group):
        x = jnp.concatenate([r[...] for r in rows[first : first + group]], axis=0)
        at_row = first * rows[0].shape[0]
        out_ref[at_row : at_row + x.shape[0], :] = jnp.dot(
            x, win_ref[pl.ds(at, half), :], preferred_element_type=F32
        )


def enter(rows, win):
    count, half = rows[0].shape
    return call(
        enter_kernel,
        [struct((len(rows) * count, win.shape[1]), F32)],
        [*rows, win],
        0,
        2 * len(rows) * count * half * win.shape[1],
    )[0]


def hide_kernel(n, *refs):
    part_ref, peer, (win_ref, wout_ref) = refs[0], refs[1 : n + 1], refs[n + 1 : n + 3]
    send, hidden_ref = refs[n + 3 : 2 * n + 3], refs[2 * n + 3]
    rows, half = peer[0].shape
    at = pl.multiple_of((1 - lax.axis_index("fsdp")) * half, 128)
    group = max(1, min(n, 256 // rows))
    for first in range(0, n, group):
        roles = range(first, min(n, first + group))
        x = jnp.concatenate([peer[r][...] for r in roles], axis=0)
        here = slice(first * rows, first * rows + x.shape[0])
        total = part_ref[here, :] + jnp.dot(
            x, win_ref[pl.ds(at, half), :], preferred_element_type=F32
        )
        hidden = jnp.maximum(total, 0.0).astype(BF16)
        hidden_ref[here, :] = hidden
        y = jnp.dot(hidden, wout_ref[:, pl.ds(at, half)], preferred_element_type=F32).astype(BF16)
        for j, r in enumerate(roles):
            send[r][...] = y[j * rows : (j + 1) * rows]


def hide(part, peer, win, wout):
    n = len(peer)
    rows, half = peer[0].shape
    outs = call(
        functools.partial(hide_kernel, n),
        [struct((rows, half))] * n + [struct(part.shape)],
        [part, *peer, win, wout],
        0,
        4 * n * rows * half * win.shape[1],
    )
    return outs[:n], outs[n]


def leave_kernel(n, hidden_ref, wout_ref, *keep):
    rows, half = keep[0].shape
    at = pl.multiple_of(lax.axis_index("fsdp") * half, 128)
    group = max(1, min(n, 256 // rows))
    for first in range(0, n, group):
        roles = range(first, min(n, first + group))
        hidden = hidden_ref[first * rows : (first + len(roles)) * rows, :]
        y = jnp.dot(hidden, wout_ref[:, pl.ds(at, half)], preferred_element_type=F32).astype(BF16)
        for j, r in enumerate(roles):
            keep[r][...] = y[j * rows : (j + 1) * rows]


def leave(hidden, wout, n):
    rows, half = hidden.shape[0] // n, wout.shape[1] // 2
    return call(
        functools.partial(leave_kernel, n),
        [struct((rows, half))] * n,
        [hidden, wout],
        0,
        2 * n * rows * half * wout.shape[0],
    )


def finish_kernel(count_ref, mine_ref, peer_ref, order_ref, score_ref, out_ref):
    rows, half = mine_ref.shape
    core = lax.axis_index("fsdp")
    pick = (iota((CAP, rows), 1) == iota((CAP, rows), 0) + core * CAP).astype(BF16)
    lanes, slot = iota((CAP, TILE), 1), iota((CAP, TILE), 0)
    order = jnp.broadcast_to(order_ref[...], (CAP, TILE))
    row = jnp.sum(jnp.where(lanes == slot, order, 0), axis=1, keepdims=True)
    score = jnp.sum(jnp.where(lanes == row, score_ref[...].astype(F32), 0.0), axis=1, keepdims=True)
    score = jnp.where(iota((CAP, 1), 0) < count_ref[...], score, 0.0)
    for ref, start in ((mine_ref, core * half), (peer_ref, (1 - core) * half)):
        y = jnp.dot(pick, ref[...], preferred_element_type=F32)
        out_ref[:, pl.ds(pl.multiple_of(start, 128), half)] = (score * y).astype(BF16)


def finish(counts, mine, peer, order, score):
    rows, half = mine.shape
    return call(
        finish_kernel,
        [struct((CAP, 2 * half))],
        [counts, mine, peer, order, score],
        0,
        4 * CAP * rows * half,
    )[0]


def load_kernel(*refs):
    n = len(refs) // 2
    copies = [pltpu.make_async_copy(refs[i], refs[n + i], refs[2 * n].at[i]) for i in range(n)]
    for c in copies:
        c.start()
    for c in copies:
        c.wait()


def load(*arrays):
    n = len(arrays)
    return pl.pallas_call(
        load_kernel,
        out_shape=[struct(a.shape, a.dtype) for a in arrays],
        in_specs=[pl.BlockSpec(memory_space=pltpu.HBM)] * n,
        out_specs=[VMEM] * n,
        scratch_shapes=[pltpu.SemaphoreType.DMA((n,))],
        cost_estimate=pl.CostEstimate(
            flops=0, bytes_accessed=sum(2 * a.size for a in arrays), transcendentals=0
        ),
        compiler_params=pltpu.CompilerParams(
            vmem_limit_bytes=42 << 20
        ),
    )(*arrays)


def total(*terms):
    return sum(t.astype(F32) for t in terms).astype(BF16)


NEAR, OTHER, DIAGONAL = (2, 1), (1, 2), (3, 3)


def routed_ffn(tokens, gain, win, wout, score, counts, order, heavy_qkv):
    devices = lax.axis_size("seq") * lax.axis_size("fsdp")
    own = pick_rows(counts, tokens, order, gain)
    win, wout = load(win, wout)
    blocks = gather_seq(own)
    peers = [swap_core(x) for x in blocks]
    x0, place = compact(blocks, peers, MEAN_LIVE * devices)
    heavy_qkv, counts_later, _ = lax.optimization_barrier((heavy_qkv, counts, x0))
    x1 = swap_doc(x0, NEAR)
    x2 = swap_doc(x0, OTHER)
    x3 = swap_doc(x1, OTHER)
    p0, p2, p1, p3 = [swap_core(x) for x in (x0, x1, x2, x3)]
    send, hidden = hide(enter((x0, x1, x2), win), (p0, p1, p2), win, wout)
    keep = leave(hidden, wout, 3)
    back = [swap_core(x) for x in send]
    got1 = swap_doc(total(keep[1], back[2]), NEAR)
    got2 = swap_doc(total(keep[2], back[1]), OTHER)
    send3, hidden = hide(enter((x3,), win), (p3,), win, wout)
    keep3 = leave(hidden, wout, 1)
    got3 = swap_doc(total(keep3[0], swap_core(send3[0])), DIAGONAL)
    summed = scatter_seq(spread(place, (keep[0], back[0], got1, got2, got3)))
    return finish(counts, summed, swap_core(summed), order, score), heavy_qkv, counts_later


def light_kernel(qkv_ref, far_ref, near_ref, out_ref):
    rows = qkv_ref.shape[1]
    core = lax.axis_index("fsdp")
    first_pos = lax.axis_index(("seq", "fsdp")) * rows
    length = rows * lax.axis_size("seq") * lax.axis_size("fsdp")
    span = rows + 2 * HALF_WIN
    lane = iota((rows, span), 1)
    row = iota((rows, span), 0)
    turn = jnp.where(core == 0, 0, rows + HALF_WIN)
    col = jnp.where(
        lane < HALF_WIN,
        lane + turn,
        jnp.where(lane < HALF_WIN + rows, lane, lane - turn),
    )
    pos = first_pos - HALF_WIN + col
    inside = (col >= row) & (col < row + 2 * HALF_WIN) & (pos >= 0) & (pos < length)
    bias = jnp.where(inside, 0.0, -1e30)
    for h in range(out_ref.shape[1] // HEAD_DIM):
        at = slice(h * HEAD_DIM, (h + 1) * HEAD_DIM)
        keys = jnp.concatenate([far_ref[0, :, at], qkv_ref[1, :, at], near_ref[0, :, at]], axis=0)
        values = jnp.concatenate([far_ref[1, :, at], qkv_ref[2, :, at], near_ref[1, :, at]], axis=0)
        s = lax.dot_general(
            qkv_ref[0, :, at], keys, (((1,), (1,)), ((), ())), preferred_element_type=F32
        )
        s = s * (1.0 / math.sqrt(HEAD_DIM)) + bias
        e = jnp.exp(s - jnp.max(s, axis=1, keepdims=True))
        y = jnp.dot(e.astype(BF16), values, preferred_element_type=F32)
        out_ref[:, at] = (y / jnp.sum(e, axis=1, keepdims=True)).astype(BF16)


def halo_kernel(planes_ref, far_ref, near_ref, sems):
    last = planes_ref.shape[1] - HALF_WIN
    edge = pl.multiple_of(lax.axis_index("fsdp") * last, HALF_WIN)
    other = pl.multiple_of(last - edge, HALF_WIN)
    copies = [
        pltpu.make_async_copy(planes_ref.at[1:3, pl.ds(at, HALF_WIN)], ref, sems.at[i])
        for i, (at, ref) in enumerate(((edge, far_ref), (other, near_ref)))
    ]
    for c in copies:
        c.start()
    for c in copies:
        c.wait()


def light_branch(planes):
    _, rows, width = planes.shape
    run = pl.pallas_call(
        halo_kernel,
        out_shape=[struct((2, HALF_WIN, width))] * 2,
        in_specs=[pl.BlockSpec(memory_space=pl.ANY)],
        out_specs=[VMEM] * 2,
        scratch_shapes=[pltpu.SemaphoreType.DMA((2,))],
        cost_estimate=pl.CostEstimate(
            flops=0, bytes_accessed=8 * HALF_WIN * width, transcendentals=0
        ),
        compiler_params=pltpu.CompilerParams(vmem_limit_bytes=48 << 20),
    )
    far, near = run(planes)
    n = lax.axis_size("seq") * lax.axis_size("fsdp")
    pairs = [(i, i + 1) for i in range(1, n - 1, 2)]
    far = lax.ppermute(far, ("seq", "fsdp"), pairs + [(j, i) for i, j in pairs])
    near = swap_core(near)
    wide = 4 * HEAD_DIM
    run = pl.pallas_call(
        light_kernel,
        out_shape=struct((rows, width)),
        grid=(width // wide,),
        in_specs=[
            pl.BlockSpec((3, rows, wide), lambda i: (0, 0, i)),
            pl.BlockSpec((2, HALF_WIN, wide), lambda i: (0, 0, i)),
            pl.BlockSpec((2, HALF_WIN, wide), lambda i: (0, 0, i)),
        ],
        out_specs=pl.BlockSpec((rows, wide), lambda i: (0, i)),
        cost_estimate=pl.CostEstimate(
            flops=4 * rows * 2 * rows * width,
            bytes_accessed=12 * rows * width,
            transcendentals=2 * rows * rows * LIGHT_HEADS,
        ),
        compiler_params=pltpu.CompilerParams(vmem_limit_bytes=12 << 20),
    )
    return run(planes, far, near)


def heavy_kernel(q_ref, near_ref, far_ref, out_ref):
    rows, width = q_ref.shape
    n = 2 * near_ref.shape[0]
    kv = jnp.concatenate([near_ref[...], far_ref[...]], axis=0)
    first = (iota((8, HEAD_DIM), 1) == 0).astype(BF16)
    marks = lax.dot_general(
        first, kv[:, :HEAD_DIM], (((1,), (1,)), ((), ())), preferred_element_type=F32
    )[0:1]
    lane, row = iota((rows, n), 1), iota((rows, n), 0)
    same = (lax.rem(lane, 2 * CAP) < CAP) == (row < CAP)
    usable = same & (marks < MARK / 2)
    for h in range(width // HEAD_DIM):
        at = slice(h * HEAD_DIM, (h + 1) * HEAD_DIM)
        s = lax.dot_general(
            q_ref[:, at], kv[:, at], (((1,), (1,)), ((), ())), preferred_element_type=F32
        )
        s = jnp.where(usable, s * (1.0 / math.sqrt(HEAD_DIM)), -1e30)
        e = jnp.exp(s - jnp.max(s, axis=1, keepdims=True))
        y = jnp.dot(
            e.astype(BF16),
            kv[:, width + h * HEAD_DIM : width + (h + 1) * HEAD_DIM],
            preferred_element_type=F32,
        )
        out_ref[:, at] = (y / jnp.sum(e, axis=1, keepdims=True)).astype(BF16)


def heavy_branch(qkv, slot_live):
    slots, _, width = qkv.shape
    half = width // 2

    def stacked(x):
        return jnp.concatenate([x[:, :half], x[:, half:]], axis=0)

    q = stacked(qkv[:, 0])
    keys = jnp.where(slot_live[:, None], qkv[:, 1], jnp.bfloat16(MARK))
    kv = jnp.concatenate([stacked(keys), stacked(qkv[:, 2])], axis=1)
    parts = gather_seq(kv)
    near = jnp.concatenate(parts, axis=0)
    far = swap_core(near)
    out = call(
        heavy_kernel,
        [struct((2 * slots, half))],
        [q, near, far],
        0,
        4 * 2 * slots * 2 * near.shape[0] * half,
    )[0]
    out = jnp.concatenate([out[:slots], out[slots:]], axis=1)
    return jnp.where(slot_live[:, None], out, jnp.bfloat16(0))


def layer(
    tokens, ffn_gain, in_proj, out_proj, router_score, tile_counts, tile_order, light_qkv, heavy_qkv
):
    assert tile_order.shape[1] == 1 and lax.axis_size("fsdp") == 2 and lax.axis_size("dp") == 4
    heavy_ffn, heavy_qkv, counts_later = routed_ffn(
        tokens[0],
        ffn_gain[None],
        in_proj,
        out_proj,
        router_score,
        tile_counts,
        tile_order[0],
        heavy_qkv,
    )
    slot_live = jnp.arange(CAP) < counts_later[0, 0]
    light_out = light_branch(jnp.transpose(light_qkv[0], (1, 0, 2)))
    heavy_attn = heavy_branch(heavy_qkv[0], slot_live)
    return (light_out[None], heavy_attn[None], heavy_ffn[None])


def solution(mesh):
    placed = (
        P("dp", ("seq", "fsdp"), None),
        P(),
        P(None, ("dp", "seq", "fsdp")),
        P(("dp", "seq", "fsdp"), None),
        P("dp", ("seq", "fsdp")),
        P("dp", ("seq", "fsdp")),
        P("dp", ("seq", "fsdp"), None),
        P("dp", ("seq", "fsdp"), None, None),
        P("dp", ("seq", "fsdp"), None, None),
    )
    return jax.shard_map(
        layer,
        mesh=mesh,
        in_specs=placed,
        out_specs=(
            P("dp", ("seq", "fsdp"), None),
            P("dp", ("seq", "fsdp"), None),
            P("dp", ("seq", "fsdp"), None),
        ),
        check_vma=False,
    )
```

```python
import functools
import math

import jax
import jax.numpy as jnp
from jax import lax
from jax.experimental import pallas as pl
from jax.experimental.pallas import tpu as pltpu
from jax.sharding import PartitionSpec as P


HEAD_DIM = 128
LIGHT_HEADS = 16
TILE = 128
CAP = 12
MEAN_LIVE = 8
HALF_WIN = 64
MARK = 1048576.0
F32, BF16 = jnp.float32, jnp.bfloat16
SCALE = math.log2(math.e) / math.sqrt(HEAD_DIM)
VMEM = pl.BlockSpec(memory_space=pltpu.VMEM)
SMEM = pl.BlockSpec(memory_space=pltpu.SMEM)


def iota(shape, dim):
    return lax.broadcasted_iota(jnp.int32, shape, dim)


def call(body, outs, args, scalars, flops, room=4 << 20, **kw):
    size = sum(math.prod(a.shape) * a.dtype.itemsize for a in (*args, *outs))
    return pl.pallas_call(
        body,
        out_shape=outs,
        in_specs=[SMEM] * scalars + [VMEM] * (len(args) - scalars),
        out_specs=[VMEM] * len(outs),
        cost_estimate=pl.CostEstimate(flops=flops, bytes_accessed=size, transcendentals=0),
        compiler_params=pltpu.CompilerParams(vmem_limit_bytes=min(60 << 20, size + room)),
        **kw,
    )(*args)


def struct(shape, dtype=BF16):
    return jax.ShapeDtypeStruct(shape, dtype)


def swap_core(x):
    return lax.ppermute(x, "fsdp", [(0, 1), (1, 0)])


def swap_seq(x, mask):
    n = lax.axis_size("seq")
    return lax.ppermute(x, "seq", [(i, i ^ mask) for i in range(n)])


def swap_doc(x, masks):
    docs = range(lax.axis_size("dp"))
    pairs = [(2 * d + c, 2 * (d ^ masks[c]) + c) for d in docs for c in range(2)]
    return lax.ppermute(x, ("dp", "fsdp"), pairs)


def seq_stages():
    n, stride, out = lax.axis_size("seq"), 1, []
    while stride < n:
        radix = min(4, n // stride)
        out.append((stride, radix))
        stride *= radix
    return out


def gather_seq(x):
    parts = [x]
    for stride, radix in seq_stages():
        x = jnp.concatenate(parts, axis=0) if len(parts) > 1 else parts[0]
        far = {k: swap_seq(x, k * stride) for k in range(radix - 1, 0, -1)}
        parts = [x] + [far[k] for k in range(1, radix)]
    return parts


def scatter_seq(parts):
    stages = seq_stages()
    for at in range(len(stages) - 1, -1, -1):
        stride, radix = stages[at]
        far = {k: swap_seq(parts[k], k * stride) for k in range(radix - 1, 0, -1)}
        total = parts[0].astype(F32)
        for k in range(1, radix):
            total = total + far[k].astype(F32)
        total = total.astype(BF16)
        if at:
            parts = jnp.split(total, stages[at - 1][1], axis=0)
    return total


def pick_kernel(count_ref, tokens_ref, order_ref, gain_ref, out_ref):
    rows, half = out_ref.shape
    slot = lax.rem(iota((rows, 1), 0), CAP)
    lanes = iota((rows, TILE), 1)
    order = jnp.broadcast_to(order_ref[...], (rows, TILE))
    row = jnp.sum(jnp.where(lanes == slot, order, 0), axis=1, keepdims=True)
    x = jnp.dot((lanes == row).astype(BF16), tokens_ref[...], preferred_element_type=F32)
    scale = lax.rsqrt(jnp.mean(x * x, axis=1, keepdims=True) + 1e-06)
    first = iota((rows, 1), 0) < CAP
    x = jnp.where(first, x[:, :half], x[:, half:])
    gain = jnp.where(first, gain_ref[:, :half], gain_ref[:, half:])
    dead = slot >= count_ref[...]
    out_ref[...] = jnp.where(dead, MARK, x * scale * gain).astype(BF16)


def pick_rows(counts, tokens, order, gain):
    rows, width = 2 * CAP, tokens.shape[1]
    return call(
        pick_kernel,
        [struct((rows, width // 2))],
        [counts, tokens, order, gain],
        0,
        2 * rows * TILE * width,
        room=54 << 20,
    )[0]


def compact_kernel(parts, *refs):
    blocks, out_ref = refs[: 2 * parts], refs[2 * parts]
    live_rows, width = out_ref.shape
    n = blocks[0].shape[0]
    core = lax.axis_index("fsdp")
    group = 2 * parts if 2 * parts * n <= 512 else 1

    def place_of(index):
        other = index >= parts * n
        index = jnp.where(other, index - parts * n, index)
        turned = jnp.where(lax.rem(index, 2 * CAP) < CAP, index + CAP, index - CAP)
        return jnp.where(other, turned, index)

    def live_of(first, data):
        index = iota((data.shape[0], 1), 0) + first * n
        usable = (lax.rem(index, 2 * CAP) < CAP) == (core == 0)
        return jnp.where(usable & (data[:, 0:128].astype(F32)[:, 0:1] < MARK / 2), 1.0, 0.0)

    starts = range(0, 2 * parts, group)
    datas = [jnp.concatenate([r[...] for r in blocks[f : f + group]], axis=0) for f in starts]
    lives = [live_of(f, d) for f, d in zip(starts, datas)]
    total = jnp.zeros((live_rows, width), F32)
    m = group * n
    up, side = iota((m, m), 0), iota((m, m), 1)
    for f, data, live in zip(starts, datas, lives):
        at = place_of(side + f * n)
        ahead = jnp.zeros((1, m), F32)
        for g, other in zip(starts, lives):
            before = jnp.where(place_of(up + g * n) < at, other, 0.0)
            ahead = ahead + jnp.sum(before, axis=0, keepdims=True)
        there = jnp.sum(jnp.where(up == side, live, 0.0), axis=0, keepdims=True)
        to_row = iota((live_rows, m), 0).astype(F32) == ahead
        pick = jnp.where(to_row & (there > 0.5), 1.0, 0.0).astype(BF16)
        total = total + jnp.dot(pick, data, preferred_element_type=F32)
    out_ref[...] = total.astype(BF16)


def compact(mine, peer, live_rows):
    n, width = mine[0].shape
    return call(
        functools.partial(compact_kernel, len(mine)),
        [struct((live_rows, width))],
        [*mine, *peer],
        0,
        4 * len(mine) * n * live_rows * width,
    )[0]


def place_kernel(parts, *refs):
    mine, peer, place_ref = refs[:parts], refs[parts : 2 * parts], refs[2 * parts]
    _, n, live_rows = place_ref.shape
    up, side = iota((n, n), 0), iota((n, n), 1)
    own = (lax.rem(iota((n, 1), 0), 2 * CAP) < CAP) == (lax.axis_index("fsdp") == 0)
    base = jnp.zeros((1, 1), F32)
    for k in range(parts):
        mark = jnp.where(
            own, mine[k][:, 0:128].astype(F32)[:, 0:1], peer[k][:, 0:128].astype(F32)[:, 0:1]
        )
        live = jnp.where(mark < MARK / 2, 1.0, 0.0)
        row = jnp.sum(jnp.where(up == side, live, 0.0), axis=0, keepdims=True)
        ahead = jnp.sum(jnp.where(side < up, row, 0.0), axis=1, keepdims=True) + base
        at = iota((n, live_rows), 1).astype(F32) == ahead
        place_ref[k, :, :] = jnp.where(at & (live > 0.5), 1.0, 0.0).astype(BF16)
        base = base + jnp.sum(live, axis=0, keepdims=True)


def place(mine, peer, live_rows):
    n = mine[0].shape[0]
    return call(
        functools.partial(place_kernel, len(mine)),
        [struct((len(mine), n, live_rows))],
        [*mine, *peer],
        0,
        4 * len(mine) * n * live_rows,
    )[0]


def spread_kernel(parts, terms, place_ref, *refs):
    rows = sum(r[...].astype(F32) for r in refs[:terms]).astype(BF16)
    for k in range(parts):
        refs[terms + k][...] = jnp.dot(
            place_ref[k, :, :], rows, preferred_element_type=F32
        ).astype(BF16)


def spread(place, terms):
    parts, n, live_rows = place.shape
    width = terms[0].shape[1]
    return call(
        functools.partial(spread_kernel, parts, len(terms)),
        [struct((n, width))] * parts,
        [place, *terms],
        0,
        2 * parts * n * live_rows * width,
    )


def enter_kernel(*refs):
    *rows, win_ref, out_ref = refs
    half = rows[0].shape[1]
    at = pl.multiple_of(lax.axis_index("fsdp") * half, 128)
    group = max(1, 256 // rows[0].shape[0])
    for first in range(0, len(rows), group):
        x = jnp.concatenate([r[...] for r in rows[first : first + group]], axis=0)
        at_row = first * rows[0].shape[0]
        out_ref[at_row : at_row + x.shape[0], :] = jnp.dot(
            x, win_ref[pl.ds(at, half), :], preferred_element_type=F32
        )


def enter(rows, win):
    count, half = rows[0].shape
    return call(
        enter_kernel,
        [struct((len(rows) * count, win.shape[1]), F32)],
        [*rows, win],
        0,
        2 * len(rows) * count * half * win.shape[1],
    )[0]


def hide_kernel(n, *refs):
    part_ref, peer, (win_ref, wout_ref) = refs[0], refs[1 : n + 1], refs[n + 1 : n + 3]
    send, hidden_ref = refs[n + 3 : 2 * n + 3], refs[2 * n + 3]
    rows, half = peer[0].shape
    at = pl.multiple_of((1 - lax.axis_index("fsdp")) * half, 128)
    group = max(1, min(n, 256 // rows))
    for first in range(0, n, group):
        roles = range(first, min(n, first + group))
        x = jnp.concatenate([peer[r][...] for r in roles], axis=0)
        here = slice(first * rows, first * rows + x.shape[0])
        total = part_ref[here, :] + jnp.dot(
            x, win_ref[pl.ds(at, half), :], preferred_element_type=F32
        )
        hidden = jnp.maximum(total, 0.0).astype(BF16)
        hidden_ref[here, :] = hidden
        y = jnp.dot(hidden, wout_ref[:, pl.ds(at, half)], preferred_element_type=F32).astype(BF16)
        for j, r in enumerate(roles):
            send[r][...] = y[j * rows : (j + 1) * rows]


def hide(part, peer, win, wout):
    n = len(peer)
    rows, half = peer[0].shape
    outs = call(
        functools.partial(hide_kernel, n),
        [struct((rows, half))] * n + [struct(part.shape)],
        [part, *peer, win, wout],
        0,
        4 * n * rows * half * win.shape[1],
    )
    return outs[:n], outs[n]


def leave_kernel(n, hidden_ref, wout_ref, *keep):
    rows, half = keep[0].shape
    at = pl.multiple_of(lax.axis_index("fsdp") * half, 128)
    group = max(1, min(n, 256 // rows))
    for first in range(0, n, group):
        roles = range(first, min(n, first + group))
        hidden = hidden_ref[first * rows : (first + len(roles)) * rows, :]
        y = jnp.dot(hidden, wout_ref[:, pl.ds(at, half)], preferred_element_type=F32).astype(BF16)
        for j, r in enumerate(roles):
            keep[r][...] = y[j * rows : (j + 1) * rows]


def leave(hidden, wout, n):
    rows, half = hidden.shape[0] // n, wout.shape[1] // 2
    return call(
        functools.partial(leave_kernel, n),
        [struct((rows, half))] * n,
        [hidden, wout],
        0,
        2 * n * rows * half * wout.shape[0],
    )


def finish_kernel(count_ref, mine_ref, peer_ref, order_ref, score_ref, out_ref):
    rows, half = mine_ref.shape
    core = lax.axis_index("fsdp")
    pick = (iota((CAP, rows), 1) == iota((CAP, rows), 0) + core * CAP).astype(BF16)
    lanes, slot = iota((CAP, TILE), 1), iota((CAP, TILE), 0)
    order = jnp.broadcast_to(order_ref[...], (CAP, TILE))
    row = jnp.sum(jnp.where(lanes == slot, order, 0), axis=1, keepdims=True)
    score = jnp.sum(jnp.where(lanes == row, score_ref[...].astype(F32), 0.0), axis=1, keepdims=True)
    score = jnp.where(iota((CAP, 1), 0) < count_ref[...], score, 0.0)
    for ref, start in ((mine_ref, core * half), (peer_ref, (1 - core) * half)):
        y = jnp.dot(pick, ref[...], preferred_element_type=F32)
        out_ref[:, pl.ds(pl.multiple_of(start, 128), half)] = (score * y).astype(BF16)


def finish(counts, mine, peer, order, score):
    rows, half = mine.shape
    return call(
        finish_kernel,
        [struct((CAP, 2 * half))],
        [counts, mine, peer, order, score],
        0,
        4 * CAP * rows * half,
    )[0]


def load_kernel(*refs):
    n = len(refs) // 2
    copies = [pltpu.make_async_copy(refs[i], refs[n + i], refs[2 * n].at[i]) for i in range(n)]
    for c in copies:
        c.start()
    for c in copies:
        c.wait()


def load(*arrays):
    n = len(arrays)
    return pl.pallas_call(
        load_kernel,
        out_shape=[struct(a.shape, a.dtype) for a in arrays],
        in_specs=[pl.BlockSpec(memory_space=pltpu.HBM)] * n,
        out_specs=[VMEM] * n,
        scratch_shapes=[pltpu.SemaphoreType.DMA((n,))],
        cost_estimate=pl.CostEstimate(
            flops=0, bytes_accessed=sum(2 * a.size for a in arrays), transcendentals=0
        ),
        compiler_params=pltpu.CompilerParams(
            vmem_limit_bytes=42 << 20
        ),
    )(*arrays)


def total(*terms):
    return sum(t.astype(F32) for t in terms).astype(BF16)


NEAR, OTHER, DIAGONAL = (2, 1), (1, 2), (3, 3)


def routed_ffn(tokens, gain, win, wout, score, counts, order, heavy_qkv):
    devices = lax.axis_size("seq") * lax.axis_size("fsdp")
    own = pick_rows(counts, tokens, order, gain)
    win, wout = load(win, wout)
    blocks = gather_seq(own)
    peers = [swap_core(x) for x in blocks]
    x0 = compact(blocks, peers, MEAN_LIVE * devices)
    heavy_qkv, counts_later, _ = lax.optimization_barrier((heavy_qkv, counts, x0))
    x1 = swap_doc(x0, NEAR)
    x2 = swap_doc(x0, OTHER)
    x3 = swap_doc(x1, OTHER)
    p0, p2, p1, p3 = [swap_core(x) for x in (x0, x1, x2, x3)]
    send, hidden = hide(enter((x0, x1, x2), win), (p0, p1, p2), win, wout)
    keep = leave(hidden, wout, 3)
    back = [swap_core(x) for x in send]
    got1 = swap_doc(total(keep[1], back[2]), NEAR)
    got2 = swap_doc(total(keep[2], back[1]), OTHER)
    send3, hidden = hide(enter((x3,), win), (p3,), win, wout)
    keep3 = leave(hidden, wout, 1)
    back_to = place(blocks, peers, MEAN_LIVE * devices)
    got3 = swap_doc(total(keep3[0], swap_core(send3[0])), DIAGONAL)
    summed = scatter_seq(spread(back_to, (keep[0], back[0], got1, got2, got3)))
    return finish(counts, summed, swap_core(summed), order, score), heavy_qkv, counts_later


def light_kernel(qkv_ref, far_ref, near_ref, out_ref):
    rows = qkv_ref.shape[1]
    core = lax.axis_index("fsdp")
    first_pos = lax.axis_index(("seq", "fsdp")) * rows
    length = rows * lax.axis_size("seq") * lax.axis_size("fsdp")
    span = rows + 2 * HALF_WIN
    lane = iota((rows, span), 1)
    row = iota((rows, span), 0)
    turn = jnp.where(core == 0, 0, rows + HALF_WIN)
    col = jnp.where(
        lane < HALF_WIN,
        lane + turn,
        jnp.where(lane < HALF_WIN + rows, lane, lane - turn),
    )
    pos = first_pos - HALF_WIN + col
    inside = (col >= row) & (col < row + 2 * HALF_WIN) & (pos >= 0) & (pos < length)
    bias = jnp.where(inside, 0.0, -1e30)
    for h in range(out_ref.shape[1] // HEAD_DIM):
        at = slice(h * HEAD_DIM, (h + 1) * HEAD_DIM)
        keys = jnp.concatenate([far_ref[0, :, at], qkv_ref[1, :, at], near_ref[0, :, at]], axis=0)
        values = jnp.concatenate([far_ref[1, :, at], qkv_ref[2, :, at], near_ref[1, :, at]], axis=0)
        s = lax.dot_general(
            qkv_ref[0, :, at], keys, (((1,), (1,)), ((), ())), preferred_element_type=F32
        )
        s = s * SCALE + bias
        e = jnp.exp2(s - jnp.max(s, axis=1, keepdims=True))
        y = jnp.dot(e.astype(BF16), values, preferred_element_type=F32)
        out_ref[:, at] = (y * (1.0 / jnp.sum(e, axis=1, keepdims=True))).astype(BF16)


def halo_kernel(planes_ref, far_ref, near_ref, sems):
    last = planes_ref.shape[1] - HALF_WIN
    edge = pl.multiple_of(lax.axis_index("fsdp") * last, HALF_WIN)
    other = pl.multiple_of(last - edge, HALF_WIN)
    copies = [
        pltpu.make_async_copy(planes_ref.at[1:3, pl.ds(at, HALF_WIN)], ref, sems.at[i])
        for i, (at, ref) in enumerate(((edge, far_ref), (other, near_ref)))
    ]
    for c in copies:
        c.start()
    for c in copies:
        c.wait()


def light_branch(planes):
    _, rows, width = planes.shape
    run = pl.pallas_call(
        halo_kernel,
        out_shape=[struct((2, HALF_WIN, width))] * 2,
        in_specs=[pl.BlockSpec(memory_space=pl.ANY)],
        out_specs=[VMEM] * 2,
        scratch_shapes=[pltpu.SemaphoreType.DMA((2,))],
        cost_estimate=pl.CostEstimate(
            flops=0, bytes_accessed=8 * HALF_WIN * width, transcendentals=0
        ),
        compiler_params=pltpu.CompilerParams(vmem_limit_bytes=48 << 20),
    )
    far, near = run(planes)
    n = lax.axis_size("seq") * lax.axis_size("fsdp")
    pairs = [(i, i + 1) for i in range(1, n - 1, 2)]
    far = lax.ppermute(far, ("seq", "fsdp"), pairs + [(j, i) for i, j in pairs])
    near = swap_core(near)
    wide = 4 * HEAD_DIM
    run = pl.pallas_call(
        light_kernel,
        out_shape=struct((rows, width)),
        grid=(width // wide,),
        in_specs=[
            pl.BlockSpec((3, rows, wide), lambda i: (0, 0, i)),
            pl.BlockSpec((2, HALF_WIN, wide), lambda i: (0, 0, i)),
            pl.BlockSpec((2, HALF_WIN, wide), lambda i: (0, 0, i)),
        ],
        out_specs=pl.BlockSpec((rows, wide), lambda i: (0, i)),
        cost_estimate=pl.CostEstimate(
            flops=4 * rows * 2 * rows * width,
            bytes_accessed=12 * rows * width,
            transcendentals=2 * rows * rows * LIGHT_HEADS,
        ),
        compiler_params=pltpu.CompilerParams(vmem_limit_bytes=12 << 20),
    )
    return run(planes, far, near)


def heavy_kernel(q_ref, near_ref, far_ref, out_ref):
    rows, width = q_ref.shape
    n = 2 * near_ref.shape[0]
    kv = jnp.concatenate([near_ref[...], far_ref[...]], axis=0)
    first = (iota((8, HEAD_DIM), 1) == 0).astype(BF16)
    marks = lax.dot_general(
        first, kv[:, :HEAD_DIM], (((1,), (1,)), ((), ())), preferred_element_type=F32
    )[0:1]
    lane, row = iota((rows, n), 1), iota((rows, n), 0)
    same = (lax.rem(lane, 2 * CAP) < CAP) == (row < CAP)
    usable = same & (marks < MARK / 2)
    for h in range(width // HEAD_DIM):
        at = slice(h * HEAD_DIM, (h + 1) * HEAD_DIM)
        s = lax.dot_general(
            q_ref[:, at], kv[:, at], (((1,), (1,)), ((), ())), preferred_element_type=F32
        )
        s = jnp.where(usable, s * SCALE, -1e30)
        e = jnp.exp2(s - jnp.max(s, axis=1, keepdims=True))
        y = jnp.dot(
            e.astype(BF16),
            kv[:, width + h * HEAD_DIM : width + (h + 1) * HEAD_DIM],
            preferred_element_type=F32,
        )
        out_ref[:, at] = (y * (1.0 / jnp.sum(e, axis=1, keepdims=True))).astype(BF16)


def heavy_branch(qkv, slot_live):
    slots, _, width = qkv.shape
    half = width // 2

    def stacked(x):
        return jnp.concatenate([x[:, :half], x[:, half:]], axis=0)

    q = stacked(qkv[:, 0])
    keys = jnp.where(slot_live[:, None], qkv[:, 1], jnp.bfloat16(MARK))
    kv = jnp.concatenate([stacked(keys), stacked(qkv[:, 2])], axis=1)
    parts = gather_seq(kv)
    near = jnp.concatenate(parts, axis=0)
    far = swap_core(near)
    out = call(
        heavy_kernel,
        [struct((2 * slots, half))],
        [q, near, far],
        0,
        4 * 2 * slots * 2 * near.shape[0] * half,
    )[0]
    out = jnp.concatenate([out[:slots], out[slots:]], axis=1)
    return jnp.where(slot_live[:, None], out, jnp.bfloat16(0))


def layer(
    tokens, ffn_gain, in_proj, out_proj, router_score, tile_counts, tile_order, light_qkv, heavy_qkv
):
    assert tile_order.shape[1] == 1 and lax.axis_size("fsdp") == 2 and lax.axis_size("dp") == 4
    heavy_ffn, heavy_qkv, counts_later = routed_ffn(
        tokens[0],
        ffn_gain[None],
        in_proj,
        out_proj,
        router_score,
        tile_counts,
        tile_order[0],
        heavy_qkv,
    )
    slot_live = jnp.arange(CAP) < counts_later[0, 0]
    light_out = light_branch(jnp.transpose(light_qkv[0], (1, 0, 2)))
    heavy_attn = heavy_branch(heavy_qkv[0], slot_live)
    return (light_out[None], heavy_attn[None], heavy_ffn[None])


def solution(mesh):
    placed = (
        P("dp", ("seq", "fsdp"), None),
        P(),
        P(None, ("dp", "seq", "fsdp")),
        P(("dp", "seq", "fsdp"), None),
        P("dp", ("seq", "fsdp")),
        P("dp", ("seq", "fsdp")),
        P("dp", ("seq", "fsdp"), None),
        P("dp", ("seq", "fsdp"), None, None),
        P("dp", ("seq", "fsdp"), None, None),
    )
    return jax.shard_map(
        layer,
        mesh=mesh,
        in_specs=placed,
        out_specs=(
            P("dp", ("seq", "fsdp"), None),
            P("dp", ("seq", "fsdp"), None),
            P("dp", ("seq", "fsdp"), None),
        ),
        check_vma=False,
    )
```

```python
import functools
import math

import jax
import jax.numpy as jnp
from jax import lax
from jax.experimental import pallas as pl
from jax.experimental.pallas import tpu as pltpu
from jax.sharding import PartitionSpec as P


HEAD_DIM = 128
LIGHT_HEADS = 16
TILE = 128
CAP = 12
MEAN_LIVE = 8
HALF_WIN = 64
MARK = 1048576.0
F32, BF16 = jnp.float32, jnp.bfloat16
SCALE = math.log2(math.e) / math.sqrt(HEAD_DIM)
VMEM = pl.BlockSpec(memory_space=pltpu.VMEM)
SMEM = pl.BlockSpec(memory_space=pltpu.SMEM)


def iota(shape, dim):
    return lax.broadcasted_iota(jnp.int32, shape, dim)


def call(body, outs, args, scalars, flops, room=4 << 20, **kw):
    size = sum(math.prod(a.shape) * a.dtype.itemsize for a in (*args, *outs))
    return pl.pallas_call(
        body,
        out_shape=outs,
        in_specs=[SMEM] * scalars + [VMEM] * (len(args) - scalars),
        out_specs=[VMEM] * len(outs),
        cost_estimate=pl.CostEstimate(flops=flops, bytes_accessed=size, transcendentals=0),
        compiler_params=pltpu.CompilerParams(vmem_limit_bytes=min(60 << 20, size + room)),
        **kw,
    )(*args)


def struct(shape, dtype=BF16):
    return jax.ShapeDtypeStruct(shape, dtype)


def swap_core(x):
    return lax.ppermute(x, "fsdp", [(0, 1), (1, 0)])


def swap_seq(x, mask):
    n = lax.axis_size("seq")
    return lax.ppermute(x, "seq", [(i, i ^ mask) for i in range(n)])


def swap_doc(x, masks):
    docs = range(lax.axis_size("dp"))
    pairs = [(2 * d + c, 2 * (d ^ masks[c]) + c) for d in docs for c in range(2)]
    return lax.ppermute(x, ("dp", "fsdp"), pairs)


def seq_stages():
    n, stride, out = lax.axis_size("seq"), 1, []
    while stride < n:
        radix = min(4, n // stride)
        out.append((stride, radix))
        stride *= radix
    return out


def gather_seq(x):
    parts = [x]
    for stride, radix in seq_stages():
        x = jnp.concatenate(parts, axis=0) if len(parts) > 1 else parts[0]
        far = {k: swap_seq(x, k * stride) for k in range(radix - 1, 0, -1)}
        parts = [x] + [far[k] for k in range(1, radix)]
    return parts


def scatter_seq(parts):
    stages = seq_stages()
    for at in range(len(stages) - 1, -1, -1):
        stride, radix = stages[at]
        far = {k: swap_seq(parts[k], k * stride) for k in range(radix - 1, 0, -1)}
        total = parts[0].astype(F32)
        for k in range(1, radix):
            total = total + far[k].astype(F32)
        total = total.astype(BF16)
        if at:
            parts = jnp.split(total, stages[at - 1][1], axis=0)
    return total


def pick_kernel(count_ref, tokens_ref, order_ref, gain_ref, out_ref):
    rows, half = out_ref.shape
    slot = lax.rem(iota((rows, 1), 0), CAP)
    lanes = iota((rows, TILE), 1)
    order = jnp.broadcast_to(order_ref[...], (rows, TILE))
    row = jnp.sum(jnp.where(lanes == slot, order, 0), axis=1, keepdims=True)
    x = jnp.dot((lanes == row).astype(BF16), tokens_ref[...], preferred_element_type=F32)
    scale = lax.rsqrt(jnp.mean(x * x, axis=1, keepdims=True) + 1e-06)
    first = iota((rows, 1), 0) < CAP
    x = jnp.where(first, x[:, :half], x[:, half:])
    gain = jnp.where(first, gain_ref[:, :half], gain_ref[:, half:])
    dead = slot >= count_ref[...]
    out_ref[...] = jnp.where(dead, MARK, x * scale * gain).astype(BF16)


def pick_rows(counts, tokens, order, gain):
    rows, width = 2 * CAP, tokens.shape[1]
    return call(
        pick_kernel,
        [struct((rows, width // 2))],
        [counts, tokens, order, gain],
        0,
        2 * rows * TILE * width,
        room=54 << 20,
    )[0]


def compact_kernel(parts, *refs):
    blocks, out_ref = refs[: 2 * parts], refs[2 * parts]
    live_rows, width = out_ref.shape
    n = blocks[0].shape[0]
    core = lax.axis_index("fsdp")
    group = 2 * parts if 2 * parts * n <= 512 else 1

    def place_of(index):
        other = index >= parts * n
        index = jnp.where(other, index - parts * n, index)
        turned = jnp.where(lax.rem(index, 2 * CAP) < CAP, index + CAP, index - CAP)
        return jnp.where(other, turned, index)

    def live_of(first, data):
        index = iota((data.shape[0], 1), 0) + first * n
        usable = (lax.rem(index, 2 * CAP) < CAP) == (core == 0)
        return jnp.where(usable & (data[:, 0:128].astype(F32)[:, 0:1] < MARK / 2), 1.0, 0.0)

    starts = range(0, 2 * parts, group)
    datas = [jnp.concatenate([r[...] for r in blocks[f : f + group]], axis=0) for f in starts]
    lives = [live_of(f, d) for f, d in zip(starts, datas)]
    total = jnp.zeros((live_rows, width), F32)
    m = group * n
    up, side = iota((m, m), 0), iota((m, m), 1)
    for f, data, live in zip(starts, datas, lives):
        at = place_of(side + f * n)
        ahead = jnp.zeros((1, m), F32)
        for g, other in zip(starts, lives):
            before = jnp.where(place_of(up + g * n) < at, other, 0.0)
            ahead = ahead + jnp.sum(before, axis=0, keepdims=True)
        there = jnp.sum(jnp.where(up == side, live, 0.0), axis=0, keepdims=True)
        to_row = iota((live_rows, m), 0).astype(F32) == ahead
        pick = jnp.where(to_row & (there > 0.5), 1.0, 0.0).astype(BF16)
        total = total + jnp.dot(pick, data, preferred_element_type=F32)
    out_ref[...] = total.astype(BF16)


def compact(mine, peer, live_rows):
    n, width = mine[0].shape
    return call(
        functools.partial(compact_kernel, len(mine)),
        [struct((live_rows, width))],
        [*mine, *peer],
        0,
        4 * len(mine) * n * live_rows * width,
    )[0]


def place_kernel(parts, *refs):
    mine, peer, place_ref = refs[:parts], refs[parts : 2 * parts], refs[2 * parts]
    n, live_rows = mine[0].shape[0], place_ref.shape[1]
    up, side = iota((n, n), 0), iota((n, n), 1)
    own = (lax.rem(iota((n, 1), 0), 2 * CAP) < CAP) == (lax.axis_index("fsdp") == 0)
    base = jnp.zeros((1, 1), F32)
    for k in range(parts):
        mark = jnp.where(
            own, mine[k][:, 0:128].astype(F32)[:, 0:1], peer[k][:, 0:128].astype(F32)[:, 0:1]
        )
        live = jnp.where(mark < MARK / 2, 1.0, 0.0)
        row = jnp.sum(jnp.where(up == side, live, 0.0), axis=0, keepdims=True)
        ahead = jnp.sum(jnp.where(side < up, row, 0.0), axis=1, keepdims=True) + base
        at = iota((n, live_rows), 1).astype(F32) == ahead
        place_ref[k * n : (k + 1) * n, :] = jnp.where(at & (live > 0.5), 1.0, 0.0).astype(BF16)
        base = base + jnp.sum(live, axis=0, keepdims=True)


def place(mine, peer, live_rows):
    n = mine[0].shape[0]
    return call(
        functools.partial(place_kernel, len(mine)),
        [struct((len(mine) * n, live_rows))],
        [*mine, *peer],
        0,
        4 * len(mine) * n * live_rows,
    )[0]


def spread_kernel(parts, terms, place_ref, *refs):
    rows = sum(r[...].astype(F32) for r in refs[:terms]).astype(BF16)
    n = refs[terms].shape[0]
    slots = jnp.dot(place_ref[...], rows, preferred_element_type=F32).astype(BF16)
    for k in range(parts):
        refs[terms + k][...] = slots[k * n : (k + 1) * n]


def spread(place, parts, terms):
    n, live_rows = place.shape[0] // parts, place.shape[1]
    width = terms[0].shape[1]
    return call(
        functools.partial(spread_kernel, parts, len(terms)),
        [struct((n, width))] * parts,
        [place, *terms],
        0,
        2 * parts * n * live_rows * width,
    )


def enter_kernel(*refs):
    *rows, win_ref, out_ref = refs
    half = rows[0].shape[1]
    at = pl.multiple_of(lax.axis_index("fsdp") * half, 128)
    group = max(1, 256 // rows[0].shape[0])
    for first in range(0, len(rows), group):
        x = jnp.concatenate([r[...] for r in rows[first : first + group]], axis=0)
        at_row = first * rows[0].shape[0]
        out_ref[at_row : at_row + x.shape[0], :] = jnp.dot(
            x, win_ref[pl.ds(at, half), :], preferred_element_type=F32
        )


def enter(rows, win):
    count, half = rows[0].shape
    return call(
        enter_kernel,
        [struct((len(rows) * count, win.shape[1]), F32)],
        [*rows, win],
        0,
        2 * len(rows) * count * half * win.shape[1],
    )[0]


def hide_kernel(n, *refs):
    part_ref, peer, (win_ref, wout_ref) = refs[0], refs[1 : n + 1], refs[n + 1 : n + 3]
    send, hidden_ref = refs[n + 3 : 2 * n + 3], refs[2 * n + 3]
    rows, half = peer[0].shape
    at = pl.multiple_of((1 - lax.axis_index("fsdp")) * half, 128)
    group = max(1, min(n, 256 // rows))
    for first in range(0, n, group):
        roles = range(first, min(n, first + group))
        x = jnp.concatenate([peer[r][...] for r in roles], axis=0)
        here = slice(first * rows, first * rows + x.shape[0])
        total = part_ref[here, :] + jnp.dot(
            x, win_ref[pl.ds(at, half), :], preferred_element_type=F32
        )
        hidden = jnp.maximum(total, 0.0).astype(BF16)
        hidden_ref[here, :] = hidden
        y = jnp.dot(hidden, wout_ref[:, pl.ds(at, half)], preferred_element_type=F32).astype(BF16)
        for j, r in enumerate(roles):
            send[r][...] = y[j * rows : (j + 1) * rows]


def hide(part, peer, win, wout):
    n = len(peer)
    rows, half = peer[0].shape
    outs = call(
        functools.partial(hide_kernel, n),
        [struct((rows, half))] * n + [struct(part.shape)],
        [part, *peer, win, wout],
        0,
        4 * n * rows * half * win.shape[1],
    )
    return outs[:n], outs[n]


def leave_kernel(n, hidden_ref, wout_ref, *keep):
    rows, half = keep[0].shape
    at = pl.multiple_of(lax.axis_index("fsdp") * half, 128)
    group = max(1, min(n, 256 // rows))
    for first in range(0, n, group):
        roles = range(first, min(n, first + group))
        hidden = hidden_ref[first * rows : (first + len(roles)) * rows, :]
        y = jnp.dot(hidden, wout_ref[:, pl.ds(at, half)], preferred_element_type=F32).astype(BF16)
        for j, r in enumerate(roles):
            keep[r][...] = y[j * rows : (j + 1) * rows]


def leave(hidden, wout, n):
    rows, half = hidden.shape[0] // n, wout.shape[1] // 2
    return call(
        functools.partial(leave_kernel, n),
        [struct((rows, half))] * n,
        [hidden, wout],
        0,
        2 * n * rows * half * wout.shape[0],
    )


def score_kernel(count_ref, order_ref, score_ref, out_ref):
    lanes, slot = iota((CAP, TILE), 1), iota((CAP, TILE), 0)
    order = jnp.broadcast_to(order_ref[...], (CAP, TILE))
    row = jnp.sum(jnp.where(lanes == slot, order, 0), axis=1, keepdims=True)
    score = jnp.sum(jnp.where(lanes == row, score_ref[...].astype(F32), 0.0), axis=1, keepdims=True)
    score = jnp.where(iota((CAP, 1), 0) < count_ref[...], score, 0.0)
    out_ref[...] = jnp.broadcast_to(score, out_ref.shape)


def finish_kernel(mine_ref, peer_ref, score_ref, out_ref):
    _, half = mine_ref.shape
    core = lax.axis_index("fsdp")
    score = score_ref[:, 0:1]
    for ref, start in ((mine_ref, core * half), (peer_ref, (1 - core) * half)):
        y = ref[...].astype(F32)
        y = jnp.where(core == 0, y[:CAP], y[CAP:])
        out_ref[:, pl.ds(pl.multiple_of(start, 128), half)] = (score * y).astype(BF16)


def finish(counts, mine, peer, order, score):
    rows, half = mine.shape
    score = call(score_kernel, [struct((CAP, TILE), F32)], [counts, order, score], 0, TILE)[0]
    return call(
        finish_kernel, [struct((CAP, 2 * half))], [mine, peer, score], 0, 4 * CAP * rows * half
    )[0]


def load_kernel(*refs):
    n = len(refs) // 2
    copies = [pltpu.make_async_copy(refs[i], refs[n + i], refs[2 * n].at[i]) for i in range(n)]
    for c in copies:
        c.start()
    for c in copies:
        c.wait()


def load(*arrays):
    n = len(arrays)
    return pl.pallas_call(
        load_kernel,
        out_shape=[struct(a.shape, a.dtype) for a in arrays],
        in_specs=[pl.BlockSpec(memory_space=pltpu.HBM)] * n,
        out_specs=[VMEM] * n,
        scratch_shapes=[pltpu.SemaphoreType.DMA((n,))],
        cost_estimate=pl.CostEstimate(
            flops=0, bytes_accessed=sum(2 * a.size for a in arrays), transcendentals=0
        ),
        compiler_params=pltpu.CompilerParams(
            vmem_limit_bytes=42 << 20
        ),
    )(*arrays)


def total(*terms):
    return sum(t.astype(F32) for t in terms).astype(BF16)


NEAR, OTHER, DIAGONAL = (2, 1), (1, 2), (3, 3)


def routed_ffn(tokens, gain, win, wout, score, counts, order, heavy_qkv):
    devices = lax.axis_size("seq") * lax.axis_size("fsdp")
    own = pick_rows(counts, tokens, order, gain)
    win, wout = load(win, wout)
    blocks = gather_seq(own)
    peers = [swap_core(x) for x in blocks]
    x0 = compact(blocks, peers, MEAN_LIVE * devices)
    heavy_qkv, counts_later, _ = lax.optimization_barrier((heavy_qkv, counts, x0))
    x1 = swap_doc(x0, NEAR)
    x2 = swap_doc(x0, OTHER)
    x3 = swap_doc(x1, OTHER)
    p0, p2, p1, p3 = [swap_core(x) for x in (x0, x1, x2, x3)]
    send, hidden = hide(enter((x0, x1, x2), win), (p0, p1, p2), win, wout)
    keep = leave(hidden, wout, 3)
    back = [swap_core(x) for x in send]
    got1 = swap_doc(total(keep[1], back[2]), NEAR)
    got2 = swap_doc(total(keep[2], back[1]), OTHER)
    send3, hidden = hide(enter((x3,), win), (p3,), win, wout)
    keep3 = leave(hidden, wout, 1)
    back_to = place(blocks, peers, MEAN_LIVE * devices)
    got3 = swap_doc(total(keep3[0], swap_core(send3[0])), DIAGONAL)
    summed = scatter_seq(spread(back_to, len(blocks), (keep[0], back[0], got1, got2, got3)))
    return finish(counts, summed, swap_core(summed), order, score), heavy_qkv, counts_later


def light_kernel(qkv_ref, far_ref, near_ref, out_ref):
    rows = qkv_ref.shape[1]
    core = lax.axis_index("fsdp")
    first_pos = lax.axis_index(("seq", "fsdp")) * rows
    length = rows * lax.axis_size("seq") * lax.axis_size("fsdp")
    span = rows + 2 * HALF_WIN
    lane = iota((rows, span), 1)
    row = iota((rows, span), 0)
    turn = jnp.where(core == 0, 0, rows + HALF_WIN)
    col = jnp.where(
        lane < HALF_WIN,
        lane + turn,
        jnp.where(lane < HALF_WIN + rows, lane, lane - turn),
    )
    pos = first_pos - HALF_WIN + col
    inside = (col >= row) & (col < row + 2 * HALF_WIN) & (pos >= 0) & (pos < length)
    bias = jnp.where(inside, 0.0, -1e30)
    for h in range(out_ref.shape[1] // HEAD_DIM):
        at = slice(h * HEAD_DIM, (h + 1) * HEAD_DIM)
        keys = jnp.concatenate([far_ref[0, :, at], qkv_ref[1, :, at], near_ref[0, :, at]], axis=0)
        values = jnp.concatenate([far_ref[1, :, at], qkv_ref[2, :, at], near_ref[1, :, at]], axis=0)
        s = lax.dot_general(
            qkv_ref[0, :, at], keys, (((1,), (1,)), ((), ())), preferred_element_type=F32
        )
        s = s * SCALE + bias
        e = jnp.exp2(s - jnp.max(s, axis=1, keepdims=True))
        y = jnp.dot(e.astype(BF16), values, preferred_element_type=F32)
        out_ref[:, at] = (y * (1.0 / jnp.sum(e, axis=1, keepdims=True))).astype(BF16)


def halo_kernel(planes_ref, far_ref, near_ref, sems):
    last = planes_ref.shape[1] - HALF_WIN
    edge = pl.multiple_of(lax.axis_index("fsdp") * last, HALF_WIN)
    other = pl.multiple_of(last - edge, HALF_WIN)
    copies = [
        pltpu.make_async_copy(planes_ref.at[1:3, pl.ds(at, HALF_WIN)], ref, sems.at[i])
        for i, (at, ref) in enumerate(((edge, far_ref), (other, near_ref)))
    ]
    for c in copies:
        c.start()
    for c in copies:
        c.wait()


def light_branch(planes):
    _, rows, width = planes.shape
    run = pl.pallas_call(
        halo_kernel,
        out_shape=[struct((2, HALF_WIN, width))] * 2,
        in_specs=[pl.BlockSpec(memory_space=pl.ANY)],
        out_specs=[VMEM] * 2,
        scratch_shapes=[pltpu.SemaphoreType.DMA((2,))],
        cost_estimate=pl.CostEstimate(
            flops=0, bytes_accessed=8 * HALF_WIN * width, transcendentals=0
        ),
        compiler_params=pltpu.CompilerParams(vmem_limit_bytes=48 << 20),
    )
    far, near = run(planes)
    n = lax.axis_size("seq") * lax.axis_size("fsdp")
    pairs = [(i, i + 1) for i in range(1, n - 1, 2)]
    far = lax.ppermute(far, ("seq", "fsdp"), pairs + [(j, i) for i, j in pairs])
    near = swap_core(near)
    wide = 8 * HEAD_DIM
    run = pl.pallas_call(
        light_kernel,
        out_shape=struct((rows, width)),
        grid=(width // wide,),
        in_specs=[
            pl.BlockSpec((3, rows, wide), lambda i: (0, 0, i)),
            pl.BlockSpec((2, HALF_WIN, wide), lambda i: (0, 0, i)),
            pl.BlockSpec((2, HALF_WIN, wide), lambda i: (0, 0, i)),
        ],
        out_specs=pl.BlockSpec((rows, wide), lambda i: (0, i)),
        cost_estimate=pl.CostEstimate(
            flops=4 * rows * 2 * rows * width,
            bytes_accessed=12 * rows * width,
            transcendentals=2 * rows * rows * LIGHT_HEADS,
        ),
        compiler_params=pltpu.CompilerParams(vmem_limit_bytes=12 << 20),
    )
    return run(planes, far, near)


def heavy_kernel(q_ref, near_ref, far_ref, out_ref):
    rows, width = q_ref.shape
    n = 2 * near_ref.shape[0]
    kv = jnp.concatenate([near_ref[...], far_ref[...]], axis=0)
    first = (iota((8, HEAD_DIM), 1) == 0).astype(BF16)
    marks = lax.dot_general(
        first, kv[:, :HEAD_DIM], (((1,), (1,)), ((), ())), preferred_element_type=F32
    )[0:1]
    lane, row = iota((rows, n), 1), iota((rows, n), 0)
    same = (lax.rem(lane, 2 * CAP) < CAP) == (row < CAP)
    usable = same & (marks < MARK / 2)
    for h in range(width // HEAD_DIM):
        at = slice(h * HEAD_DIM, (h + 1) * HEAD_DIM)
        s = lax.dot_general(
            q_ref[:, at], kv[:, at], (((1,), (1,)), ((), ())), preferred_element_type=F32
        )
        s = jnp.where(usable, s * SCALE, -1e30)
        e = jnp.exp2(s - jnp.max(s, axis=1, keepdims=True))
        y = jnp.dot(
            e.astype(BF16),
            kv[:, width + h * HEAD_DIM : width + (h + 1) * HEAD_DIM],
            preferred_element_type=F32,
        )
        out_ref[:, at] = (y * (1.0 / jnp.sum(e, axis=1, keepdims=True))).astype(BF16)


def heavy_branch(qkv, slot_live):
    slots, _, width = qkv.shape
    half = width // 2

    def stacked(x):
        return jnp.concatenate([x[:, :half], x[:, half:]], axis=0)

    q = stacked(qkv[:, 0])
    keys = jnp.where(slot_live[:, None], qkv[:, 1], jnp.bfloat16(MARK))
    kv = jnp.concatenate([stacked(keys), stacked(qkv[:, 2])], axis=1)
    parts = gather_seq(kv)
    near = jnp.concatenate(parts, axis=0)
    far = swap_core(near)
    out = call(
        heavy_kernel,
        [struct((2 * slots, half))],
        [q, near, far],
        0,
        4 * 2 * slots * 2 * near.shape[0] * half,
    )[0]
    out = jnp.concatenate([out[:slots], out[slots:]], axis=1)
    return jnp.where(slot_live[:, None], out, jnp.bfloat16(0))


def layer(
    tokens, ffn_gain, in_proj, out_proj, router_score, tile_counts, tile_order, light_qkv, heavy_qkv
):
    assert tile_order.shape[1] == 1 and lax.axis_size("fsdp") == 2 and lax.axis_size("dp") == 4
    heavy_ffn, heavy_qkv, counts_later = routed_ffn(
        tokens[0],
        ffn_gain[None],
        in_proj,
        out_proj,
        router_score,
        tile_counts,
        tile_order[0],
        heavy_qkv,
    )
    slot_live = jnp.arange(CAP) < counts_later[0, 0]
    light_out = light_branch(jnp.transpose(light_qkv[0], (1, 0, 2)))
    heavy_attn = heavy_branch(heavy_qkv[0], slot_live)
    return (light_out[None], heavy_attn[None], heavy_ffn[None])


def solution(mesh):
    placed = (
        P("dp", ("seq", "fsdp"), None),
        P(),
        P(None, ("dp", "seq", "fsdp")),
        P(("dp", "seq", "fsdp"), None),
        P("dp", ("seq", "fsdp")),
        P("dp", ("seq", "fsdp")),
        P("dp", ("seq", "fsdp"), None),
        P("dp", ("seq", "fsdp"), None, None),
        P("dp", ("seq", "fsdp"), None, None),
    )
    return jax.shard_map(
        layer,
        mesh=mesh,
        in_specs=placed,
        out_specs=(
            P("dp", ("seq", "fsdp"), None),
            P("dp", ("seq", "fsdp"), None),
            P("dp", ("seq", "fsdp"), None),
        ),
        check_vma=False,
    )
```
